32 devices in a mesh: groups: 2 (over y), trace: 4 (over z), space: 2 (over x), sub: 2 (over core).
Axes of the slice: x: 2, y: 2, z: 4, core: 2. Of those that a mesh axis runs over, the one named last changes fastest.
Arguments:
- seismic: bfloat16 [256, 1024, 128], P(('groups', 'trace', 'space', 'sub')), parts along dimension 0, may hold values from -6 to 6
- band_low: int32 [256], P('groups'), parts along dimension 0, may hold values from 0 to 127
- band_high: int32 [256], P('groups'), parts along dimension 0, may hold values from 256 to 512
- leaf_weights: bfloat16 [8, 512, 2, 64], replicated, may hold values from -0.15625 to 0.15625
- translations: float32 [32, 2, 64, 64], replicated, may hold values from -1 to 1
- level_table: int32 [3, 8, 2], replicated, may hold values from 0 to 31
Outputs:
- image_weights: float32 [16, 2, 64, 128], P(('groups', 'trace', 'space'), None, 'sub'), parts along dimension 0
The draws below stay inside these ranges and needn't reach their ends.
There are 2 independent parts, one for each index of `groups`. The reference program is written for one: setup_inputs(seed, part) draws one part's arguments, and reference() takes and returns one part's arrays. A program takes and returns all parts, laid end to end along the dimension named above; an argument that names none is the same for every part. Nothing has to cross between parts.
All inputs are finite; a program needn't handle non-finite values.
Results may differ from the reference program's by a relative error of at most 0.0037.
Values may be sent and summed in bfloat16 or wider, within the bound.
No kernel may reach another device: no remote copies, remote signals or barrier semaphores. Data moves between devices by JAX's collectives and lax.ppermute only.
A program may use at most 64 MiB of HBM per device.

```python
import math
import jax
import jax.numpy as jnp
from jax import lax

SHOTS = 128
TR_DEV = 8
NT = 1024
F = 512
R = 64
NMAT = 32
TRACES = 128
NBOX = 8
SPACE_BITS = 1
TRACE_BITS = 2
LEVEL_ROWS = 3
N_TRACE = 4
N_SPACE = 2
N_SUB = 2


def set_ends(array, key, smallest, high):
    longest = array.shape.index(max(array.shape))
    spots = []
    for shift in (0, 1):
        where = [jax.random.randint(jax.random.fold_in(key, axis), (), 0, length) for axis, length in enumerate(array.shape)]
        where[longest] = (where[longest] + shift) % array.shape[longest]
        spots.append(tuple(where))
    return array.at[spots[0]].set(smallest).at[spots[1]].set(high)


def steps_of(own_key, extent, split, low, high):
    loudness = 1.0
    for dim, blocks in split:
        draws = jax.random.uniform(jax.random.fold_in(jax.random.fold_in(own_key, 6), dim), (blocks,), jnp.float32, low / len(split), high / len(split))
        loudness = loudness * jnp.repeat(jnp.exp(draws), extent[dim] // blocks).reshape((-1,) + (1,) * (len(extent) - 1 - dim))
    return loudness


def gaussian(stream_key, shape, scale, reach, split=(), held_as=jnp.bfloat16):
    values = scale * jax.random.normal(stream_key, shape, jnp.float32)
    if split:
        values = values * steps_of(stream_key, shape, split, -0.22, 0.18)
    return jnp.clip(values, -reach, reach).astype(held_as)


def setup_inputs(seed: int = 0, part: int = 0) -> dict:
    key_of = jax.random.split(jax.random.key(seed), 7)
    part_splits = jax.random.split(jax.random.fold_in(key_of[6], part), 7)
    return {
        "seismic": gaussian(part_splits[0], (TRACES, NT, SHOTS), 1.0, 6.0, ((0, 16),)),
        "band_low": set_ends(jax.random.randint(part_splits[1], (SHOTS,), 0, F // 4), jax.random.fold_in(part_splits[1], 1), 0, (F // 4) - 1).astype(jnp.int32),
        "band_high": set_ends(jax.random.randint(part_splits[2], (SHOTS,), F // 2, F + 1), jax.random.fold_in(part_splits[2], 1), F // 2, F).astype(jnp.int32),
        "leaf_weights": gaussian(key_of[3], (TR_DEV, F, 2, R), (1.0 / (TR_DEV * N_TRACE * N_SUB * (F // N_TRACE)) ** 0.5), 0.15625),
        "translations": gaussian(key_of[4], (NMAT, 2, R, R), (0.5 / R ** 0.5), 1.0, (), jnp.float32),
        "level_table": set_ends(jax.random.randint(key_of[5], (LEVEL_ROWS, NBOX, 2), 0, NMAT), jax.random.fold_in(key_of[5], 1), 0, NMAT - 1).astype(jnp.int32),
    }


def spectral_table(freq_total, samples):
    freq_range = jnp.arange(freq_total, dtype=jnp.int32)
    time_range = jnp.arange(samples, dtype=jnp.int32)
    phase = freq_range[:, None] * time_range[None, :] % samples
    angle = phase.astype(jnp.float32) * (2.0 * math.pi / samples)
    factor = 1.0 / math.sqrt(samples)
    return (jnp.concatenate([jnp.cos(angle), -jnp.sin(angle)], axis=0) * factor).astype(jnp.bfloat16)

def complex_product(left, right):
    highest = lax.Precision.HIGHEST
    real_part = jnp.dot(left[0], right[0], precision=highest) - jnp.dot(left[1], right[1], precision=highest)
    imag_part = jnp.dot(left[0], right[1], precision=highest) + jnp.dot(left[1], right[0], precision=highest)
    return jnp.stack([real_part, imag_part])

def reference(seismic, band_low, band_high, leaf_weights, translations, level_table):
    highest = lax.Precision.HIGHEST
    dft_rows = spectral_table(F, NT)
    dft_wide = dft_rows.astype(jnp.float32)
    freq_index = jnp.arange(F, dtype=jnp.int32)
    band_mask = ((freq_index[:, None] >= band_low[None, :]) & (freq_index[:, None] < band_high[None, :])).astype(jnp.bfloat16)
    blocks = seismic.reshape(N_TRACE, N_SPACE, N_SUB, TR_DEV, NT, SHOTS)

    def accumulate(carry, block):
        spectra = jnp.einsum('kt,puxts->puxks', dft_wide, block.astype(jnp.float32), precision=highest)
        spectra = spectra.astype(jnp.bfloat16).reshape(N_SPACE, N_SUB, TR_DEV, 2, F, SHOTS) * band_mask
        return (carry + lax.optimization_barrier(jnp.sum(spectra.astype(jnp.float32), axis=1)), None)
    start_sum = jnp.zeros((N_SPACE, TR_DEV, 2, F, SHOTS), jnp.float32)
    summed, _ = lax.scan(accumulate, start_sum, blocks)
    freq_block = F // N_TRACE
    banded = summed.reshape(N_SPACE, TR_DEV, 2, N_TRACE, freq_block, SHOTS)
    leaf_wide = leaf_weights.astype(jnp.float32).reshape(TR_DEV, N_TRACE, freq_block, 2, R)
    parts = jnp.einsum('piagfs,igfbr->gpabrs', banded, leaf_wide, precision=highest)
    real_part = parts[:, :, 0, 0] - parts[:, :, 1, 1]
    imag_part = parts[:, :, 0, 1] + parts[:, :, 1, 0]
    weights_now = jnp.stack([real_part, imag_part], axis=2).reshape(N_TRACE * N_SPACE, 2, R, SHOTS)
    box_index = jnp.arange(N_TRACE * N_SPACE, dtype=jnp.int32)
    for section_no in range(SPACE_BITS + TRACE_BITS):
        stride = 2 ** section_no
        lower_box = box_index - box_index // stride % 2 * stride
        upper_box = lower_box + stride
        first_mats = translations[level_table[section_no, :, 0]]
        second_mats = translations[level_table[section_no, :, 1]]
        weights_now = jax.vmap(complex_product)(first_mats, weights_now[lower_box]) + jax.vmap(complex_product)(second_mats, weights_now[upper_box])
    return weights_now
```

```python
import functools
import math

import jax
import jax.numpy as jnp
import numpy as np
from jax import lax
from jax.experimental import pallas as pl
from jax.experimental.pallas import tpu as pltpu
from jax.sharding import PartitionSpec as P

CHUNK = 128


def spectral_rows(freq_total, samples, chunk):
    phase = (np.arange(freq_total)[:, None] * np.arange(samples)[None, :]) % samples
    angle = phase.astype(np.float32) * np.float32(2.0 * math.pi / samples)
    factor = np.float32(1.0 / math.sqrt(samples))
    rows = np.stack([np.cos(angle) * factor, -np.sin(angle) * factor])
    rows = rows.reshape(2, freq_total // chunk, chunk, samples).swapaxes(0, 1)
    return rows.reshape(freq_total // chunk, 2 * chunk, samples).astype(jnp.bfloat16)


def halves(x):
    high = x.astype(jnp.bfloat16)
    return high, (x - high.astype(jnp.float32)).astype(jnp.bfloat16)


def reversed_bits(index, bits):
    out = 0
    for bit in range(bits):
        out = out | (((index >> bit) & 1) << (bits - 1 - bit))
    return out


def source_kernel(
    sizes,
    place_ref,
    table_ref,
    low_ref,
    high_ref,
    seismic_hbm,
    rows_hbm,
    leaf_hbm,
    moves_hbm,
    keep_ref,
    send_ref,
    seismic_ref,
    rows_ref,
    leaf_ref,
    moves_ref,
    spectra_ref,
    now_ref,
    next_ref,
    sems,
):
    traces, samples, shots, freq_total, rank, bands, spaces, subs = sizes
    chunks = freq_total // CHUNK
    freq_block = freq_total // bands
    boxes = bands * spaces
    box_bits = boxes.bit_length() - 1
    sub_bits = subs.bit_length() - 1
    space_bits = spaces.bit_length() - 1
    part = rank // subs
    own_box, own_space, own_sub = place_ref[0], place_ref[1], place_ref[2]

    copies = []
    for source, target in (
        [(rows_hbm.at[0], rows_ref.at[0])]
        + [(seismic_hbm.at[j], seismic_ref.at[j]) for j in range(traces)]
        + [(leaf_hbm, leaf_ref)]
        + [(rows_hbm.at[c], rows_ref.at[c]) for c in range(1, chunks)]
        + [(moves_hbm, moves_ref)]
    ):
        copy = pltpu.make_async_copy(source, target, sems.at[len(copies)])
        copy.start()
        copies.append(copy)
    copies[0].wait()

    for c in range(chunks):
        if c > 0:
            copies[traces + 1 + c].wait()
        freq = lax.broadcasted_iota(jnp.int32, (CHUNK, shots), 0) + c * CHUNK
        kept = (freq >= low_ref[...]) & (freq < high_ref[...])
        for j in range(0, traces, 2):
            if c == 0:
                copies[1 + j].wait()
                copies[2 + j].wait()
            pair = jnp.concatenate([seismic_ref[j], seismic_ref[j + 1]], axis=1)
            spectra = jnp.dot(rows_ref[c], pair, preferred_element_type=jnp.float32)
            for k in range(2):
                cut = spectra[:, k * shots : (k + 1) * shots]
                for part_no in range(2):
                    piece = cut[part_no * CHUNK : (part_no + 1) * CHUNK]
                    piece = jnp.where(kept, piece, 0.0).astype(jnp.bfloat16)
                    spectra_ref[c, pl.ds((j + k) * CHUNK, CHUNK), pl.ds(part_no * shots, shots)] = piece
    copies[traces + 1].wait()
    copies[traces + 1 + chunks].wait()
    for g in range(bands):
        first = g * freq_block
        total = None
        for start in range(first, first + freq_block, min(freq_block, CHUNK)):
            c, offset = start // CHUNK, start % CHUNK
            width = min(freq_block, CHUNK)
            for j in range(traces):
                term = jnp.dot(
                    leaf_ref[j, :, pl.ds(start, width)],
                    spectra_ref[c, pl.ds(j * CHUNK + offset, width), :],
                    preferred_element_type=jnp.float32,
                )
                total = term if total is None else total + term
        now_ref[g, :rank] = total[:rank, :shots] - total[rank:, shots:]
        now_ref[g, rank:] = total[rank:, :shots] + total[:rank, shots:]

    def complex_rows(entry):
        real, imag = moves_ref[entry, 0], moves_ref[entry, 1]
        return jnp.concatenate(
            [jnp.concatenate([real, -imag], axis=1), jnp.concatenate([imag, real], axis=1)], axis=0
        )

    def level(section_no, source, store):
        stride = 1 << section_no
        inside = section_no < space_bits
        count = boxes // 2 if not inside else bands * (1 << section_no)

        def body(i, carry):
            if inside:
                done = i % stride
                band = i // stride
                above = (own_space >> (section_no + 1)) << (section_no + 1)
                lower = band * spaces + above + done
                own_bit = (own_space >> section_no) & 1
                right = source[i]
                mats = [
                    complex_rows(table_ref[(section_no * boxes + lower + upper * stride) * 2 + own_bit])
                    for upper in range(2)
                ]
                places = [band * (2 * stride) + upper * stride + done for upper in range(2)]
            else:
                lower = (i // stride) * (2 * stride) + i % stride
                right = jnp.concatenate([source[lower], source[lower + stride]], axis=0)
                mats = [
                    jnp.concatenate(
                        [
                            complex_rows(table_ref[(section_no * boxes + lower + upper * stride) * 2 + child])
                            for child in range(2)
                        ],
                        axis=1,
                    )
                    for upper in range(2)
                ]
                places = [lower, lower + stride]
            left_high, left_low = halves(jnp.concatenate(mats, axis=0))
            right_high, right_low = halves(right)
            left = jnp.concatenate([left_high, left_low], axis=0)
            wide = jnp.concatenate([right_high, right_low], axis=1)
            product = jnp.dot(left, wide, preferred_element_type=jnp.float32)
            product = product[:, :shots] + product[:, shots:]
            product = product[: 4 * rank] + product[4 * rank :]
            for upper in range(2):
                store(places[upper], product[upper * 2 * rank : (upper + 1) * 2 * rank])
            return carry

        lax.fori_loop(0, count, body, 0, unroll=count <= 4)

    def store_last(box, value):
        place = reversed_bits(box ^ own_box, box_bits)
        for half in range(subs):
            across = reversed_bits(half ^ own_sub, sub_bits)
            rows = jnp.stack([value[half * part : (half + 1) * part], value[rank + half * part : rank + (half + 1) * part]])

            @pl.when(across < subs // 2)
            def _():
                keep_ref[across * boxes + place] = rows

            @pl.when(across >= subs // 2)
            def _():
                send_ref[(across - subs // 2) * boxes + place] = rows.astype(jnp.bfloat16)

    def store_in(ref):
        def store(box, value):
            ref[box] = value

        return store

    sources = [now_ref, next_ref]
    for section_no in range(box_bits):
        last = section_no == box_bits - 1
        level(section_no, sources[section_no % 2], store_last if last else store_in(sources[(section_no + 1) % 2]))


def per_device(seismic, band_low, band_high, leaf_weights, translations, level_table):
    bands, spaces, subs = (lax.axis_size(name) for name in ("trace", "space", "sub"))
    traces, samples, shots = seismic.shape
    freq_total, rank = leaf_weights.shape[1], leaf_weights.shape[3]
    boxes = bands * spaces
    chunks = freq_total // CHUNK
    own_space = lax.axis_index("space")
    own_box = lax.axis_index("trace") * spaces + own_space
    place = jnp.stack([own_box, own_space, lax.axis_index("sub")]).astype(jnp.int32)
    rows = jnp.asarray(spectral_rows(freq_total, samples, CHUNK))
    leaf = leaf_weights.transpose(0, 2, 3, 1).reshape(traces, 2 * rank, freq_total)
    out_rows = subs // 2 * boxes
    tail = (2, rank // subs, shots)
    smem = pl.BlockSpec(memory_space=pltpu.SMEM)
    vmem = pl.BlockSpec(memory_space=pltpu.VMEM)
    anywhere = pl.BlockSpec(memory_space=pl.ANY)
    keep, send = pl.pallas_call(
        functools.partial(source_kernel, (traces, samples, shots, freq_total, rank, bands, spaces, subs)),
        out_shape=(
            jax.ShapeDtypeStruct((out_rows,) + tail, jnp.float32),
            jax.ShapeDtypeStruct((out_rows,) + tail, jnp.bfloat16),
        ),
        in_specs=[smem, smem, vmem, vmem] + [anywhere] * 4,
        out_specs=(vmem, vmem),
        scratch_shapes=[
            pltpu.VMEM(seismic.shape, jnp.bfloat16),
            pltpu.VMEM(rows.shape, jnp.bfloat16),
            pltpu.VMEM(leaf.shape, jnp.bfloat16),
            pltpu.VMEM(translations.shape, jnp.float32),
            pltpu.VMEM((chunks, traces * CHUNK, 2 * shots), jnp.bfloat16),
            pltpu.VMEM((boxes, 2 * rank, shots), jnp.float32),
            pltpu.VMEM((boxes, 2 * rank, shots), jnp.float32),
            pltpu.SemaphoreType.DMA((traces + chunks + 2,)),
        ],
        name="source",
    )(
        place,
        level_table.reshape(-1),
        band_low[None, :],
        band_high[None, :],
        seismic,
        rows,
        leaf,
        translations,
    )

    def swapped(x, axis, bit):
        return lax.ppermute(x, axis, [(i, i ^ 1 << bit) for i in range(lax.axis_size(axis))])

    steps = [(axis, bit) for axis in ("sub", "space", "trace") for bit in range(lax.axis_size(axis).bit_length() - 1)]
    for axis, bit in steps:
        total = keep + swapped(send, axis, bit).astype(jnp.float32)
        half = total.shape[0] // 2
        keep, send = total[:half], total[half:].astype(jnp.bfloat16)
    return total


def solution(mesh):
    placed = (
        P(("groups", "trace", "space", "sub"), None, None),
        P("groups"),
        P("groups"),
        P(),
        P(),
        P(),
    )
    return jax.shard_map(
        per_device,
        mesh=mesh,
        in_specs=placed,
        out_specs=P(("groups", "trace", "space"), None, "sub", None),
        check_vma=False,
    )
```

```python
import functools
import math

import jax
import jax.numpy as jnp
import numpy as np
from jax import lax
from jax.experimental import pallas as pl
from jax.experimental.pallas import tpu as pltpu
from jax.sharding import PartitionSpec as P


CHUNK = 128


def spectral_rows(freq_total, samples, chunk):
    phase = (np.arange(freq_total)[:, None] * np.arange(samples)[None, :]) % samples
    angle = phase.astype(np.float32) * np.float32(2.0 * math.pi / samples)
    factor = np.float32(1.0 / math.sqrt(samples))
    rows = np.stack([np.cos(angle) * factor, -np.sin(angle) * factor])
    rows = rows.reshape(2, freq_total // chunk, chunk, samples).swapaxes(0, 1)
    return rows.reshape(freq_total // chunk, 2 * chunk, samples).astype(jnp.bfloat16)


def halves(x):
    high = x.astype(jnp.bfloat16)
    return high, (x - high.astype(jnp.float32)).astype(jnp.bfloat16)


def exchange_groups(spaces, bands):
    space_bits, band_bits = spaces.bit_length() - 1, bands.bit_length() - 1
    bits = list(range(space_bits + band_bits))
    first = [bit for bit in (0, space_bits) if bit in bits and (bit == 0 or band_bits)]
    first = sorted(set(first))
    return [first] + [[bit] for bit in bits if bit not in first]


def place_of(delta, groups):
    order = [bit for group in groups for bit in group]
    place = 0
    for k, bit in enumerate(order):
        place = place | (((delta >> bit) & 1) << (len(order) - 1 - k))
    crossings = 0
    for group in groups:
        met = 0
        for bit in group:
            met = met | ((delta >> bit) & 1)
        crossings = crossings ^ met
    return place, crossings


def source_kernel(
    sizes,
    table_ref,
    low_ref,
    high_ref,
    seismic_hbm,
    rows_hbm,
    leaf_hbm,
    moves_hbm,
    keep_ref,
    send_ref,
    seismic_ref,
    rows_ref,
    leaf_ref,
    moves_ref,
    spectra_ref,
    now_ref,
    next_ref,
    sems,
):
    traces, samples, shots, freq_total, rank, bands, spaces, subs = sizes
    chunks = freq_total // CHUNK
    freq_block = freq_total // bands
    boxes = bands * spaces
    box_bits = boxes.bit_length() - 1
    space_bits = spaces.bit_length() - 1
    part = rank // subs
    groups = exchange_groups(spaces, bands)
    own_space, own_sub = lax.axis_index("space"), lax.axis_index("sub")
    own_box = lax.axis_index("trace") * spaces + own_space

    copies = []
    for source, target in (
        [(rows_hbm.at[0], rows_ref.at[0])]
        + [(seismic_hbm.at[j], seismic_ref.at[j]) for j in range(traces)]
        + [(leaf_hbm, leaf_ref)]
        + [(rows_hbm.at[c], rows_ref.at[c]) for c in range(1, chunks)]
        + [(moves_hbm, moves_ref)]
    ):
        copy = pltpu.make_async_copy(source, target, sems.at[len(copies)])
        copy.start()
        copies.append(copy)
    copies[0].wait()

    for c in range(chunks):
        if c > 0:
            copies[traces + 1 + c].wait()
        freq = lax.broadcasted_iota(jnp.int32, (CHUNK, shots), 0) + c * CHUNK
        kept = (freq >= low_ref[...]) & (freq < high_ref[...])
        for j in range(0, traces, 2):
            if c == 0:
                copies[1 + j].wait()
                copies[2 + j].wait()
            pair = jnp.concatenate([seismic_ref[j], seismic_ref[j + 1]], axis=1)
            spectra = jnp.dot(rows_ref[c], pair, preferred_element_type=jnp.float32)
            for k in range(2):
                cut = spectra[:, k * shots : (k + 1) * shots]
                for part_no in range(2):
                    piece = cut[part_no * CHUNK : (part_no + 1) * CHUNK]
                    piece = jnp.where(kept, piece, 0.0).astype(jnp.bfloat16)
                    spectra_ref[c, pl.ds((j + k) * CHUNK, CHUNK), pl.ds(part_no * shots, shots)] = piece
    copies[traces + 1].wait()
    copies[traces + 1 + chunks].wait()
    for g in range(bands):
        first = g * freq_block
        total = None
        for start in range(first, first + freq_block, min(freq_block, CHUNK)):
            c, offset = start // CHUNK, start % CHUNK
            width = min(freq_block, CHUNK)
            for j in range(traces):
                term = jnp.dot(
                    leaf_ref[j, :, pl.ds(start, width)],
                    spectra_ref[c, pl.ds(j * CHUNK + offset, width), :],
                    preferred_element_type=jnp.float32,
                )
                total = term if total is None else total + term
        now_ref[g, :rank] = total[:rank, :shots] - total[rank:, shots:]
        now_ref[g, rank:] = total[rank:, :shots] + total[:rank, shots:]

    def complex_rows(entry):
        real, imag = moves_ref[entry, 0], moves_ref[entry, 1]
        return jnp.concatenate(
            [jnp.concatenate([real, -imag], axis=1), jnp.concatenate([imag, real], axis=1)], axis=0
        )

    def level(section_no, source, store):
        stride = 1 << section_no
        inside = section_no < space_bits
        count = boxes // 2 if not inside else bands * (1 << section_no)

        def body(i, carry):
            if inside:
                done = i % stride
                band = i // stride
                above = (own_space >> (section_no + 1)) << (section_no + 1)
                lower = band * spaces + above + done
                own_bit = (own_space >> section_no) & 1
                right = source[i]
                mats = [
                    complex_rows(table_ref[section_no, own_bit, lower + upper * stride])
                    for upper in range(2)
                ]
                places = [band * (2 * stride) + upper * stride + done for upper in range(2)]
            else:
                lower = (i // stride) * (2 * stride) + i % stride
                right = jnp.concatenate([source[lower], source[lower + stride]], axis=0)
                mats = [
                    jnp.concatenate(
                        [
                            complex_rows(table_ref[section_no, child, lower + upper * stride])
                            for child in range(2)
                        ],
                        axis=1,
                    )
                    for upper in range(2)
                ]
                places = [lower, lower + stride]
            left_high, left_low = halves(jnp.concatenate(mats, axis=0))
            right_high, right_low = halves(right)
            left = jnp.concatenate([left_high, left_low], axis=0)
            wide = jnp.concatenate([right_high, right_low], axis=1)
            product = jnp.dot(left, wide, preferred_element_type=jnp.float32)
            product = product[:, :shots] + product[:, shots:]
            product = product[: 4 * rank] + product[4 * rank :]
            for upper in range(2):
                store(places[upper], product[upper * 2 * rank : (upper + 1) * 2 * rank])
            return carry

        lax.fori_loop(0, count, body, 0, unroll=count <= 4)

    def store_last(box, value):
        place, crossings = place_of(box ^ own_box, groups)
        first, second = (
            jnp.stack([value[half * part : (half + 1) * part], value[rank + half * part : rank + (half + 1) * part]])
            for half in range(2)
        )
        keep_first = (own_sub ^ crossings) == 0
        keep_ref[place] = jnp.where(keep_first, first, second)
        send_ref[place] = jnp.where(keep_first, second, first).astype(jnp.bfloat16)

    def store_in(ref):
        def store(box, value):
            ref[box] = value

        return store

    sources = [now_ref, next_ref]
    for section_no in range(box_bits):
        last = section_no == box_bits - 1
        level(section_no, sources[section_no % 2], store_last if last else store_in(sources[(section_no + 1) % 2]))


def per_device(seismic, band_low, band_high, leaf_weights, translations, level_table):
    bands, spaces, subs = (lax.axis_size(name) for name in ("trace", "space", "sub"))
    traces, samples, shots = seismic.shape
    freq_total, rank = leaf_weights.shape[1], leaf_weights.shape[3]
    boxes = bands * spaces
    chunks = freq_total // CHUNK
    rows = jnp.asarray(spectral_rows(freq_total, samples, CHUNK))
    leaf = leaf_weights.transpose(0, 2, 3, 1).reshape(traces, 2 * rank, freq_total)
    tail = (2, rank // subs, shots)
    kind = pltpu.VMEM if boxes * 2 * rank * shots <= 1 << 18 else jax.ShapeDtypeStruct
    smem = pl.BlockSpec(memory_space=pltpu.SMEM)
    vmem = pl.BlockSpec(memory_space=pltpu.VMEM)
    anywhere = pl.BlockSpec(memory_space=pl.ANY)
    keep, send = pl.pallas_call(
        functools.partial(source_kernel, (traces, samples, shots, freq_total, rank, bands, spaces, subs)),
        out_shape=(
            kind((boxes,) + tail, jnp.float32),
            kind((boxes,) + tail, jnp.bfloat16),
        ),
        in_specs=[smem, vmem, vmem] + [anywhere] * 4,
        out_specs=(vmem, vmem),
        scratch_shapes=[
            pltpu.VMEM(seismic.shape, jnp.bfloat16),
            pltpu.VMEM(rows.shape, jnp.bfloat16),
            pltpu.VMEM(leaf.shape, jnp.bfloat16),
            pltpu.VMEM(translations.shape, jnp.float32),
            pltpu.VMEM((chunks, traces * CHUNK, 2 * shots), jnp.bfloat16),
            pltpu.VMEM((boxes, 2 * rank, shots), jnp.float32),
            pltpu.VMEM((boxes, 2 * rank, shots), jnp.float32),
            pltpu.SemaphoreType.DMA((traces + chunks + 2,)),
        ],
        name="source",
    )(
        level_table.transpose(0, 2, 1),
        band_low[None, :],
        band_high[None, :],
        seismic,
        rows,
        leaf,
        translations,
    )

    axes = ("trace", "space", "sub")

    def swapped(x, mask, flip):
        return lax.ppermute(x, axes, [(i, ((i >> 1 ^ mask) << 1) | (i & 1 ^ flip)) for i in range(2 * boxes)])

    total = keep + swapped(send, 0, 1).astype(jnp.float32)
    for group in exchange_groups(spaces, bands):
        count = 1 << len(group)
        shares = total.reshape((count, -1) + tail)
        total = shares[0]
        for share in range(count - 1, 0, -1):
            mask = sum(1 << bit for k, bit in enumerate(group) if share >> (len(group) - 1 - k) & 1)
            total = total + swapped(shares[share].astype(jnp.bfloat16), mask, 1).astype(jnp.float32)
    return total


def solution(mesh):
    placed = (
        P(("groups", "trace", "space", "sub"), None, None),
        P("groups"),
        P("groups"),
        P(),
        P(),
        P(),
    )
    return jax.shard_map(
        per_device,
        mesh=mesh,
        in_specs=placed,
        out_specs=P(("groups", "trace", "space"), None, "sub", None),
        check_vma=False,
    )
```

```python
import functools
import math

import jax
import jax.numpy as jnp
import numpy as np
from jax import lax
from jax.experimental import pallas as pl
from jax.experimental.pallas import tpu as pltpu
from jax.sharding import PartitionSpec as P


def spectral_rows(freq_total, samples):
    quarter = freq_total // 4
    phase = (np.arange(quarter)[:, None] * np.arange(samples)[None, :]) % samples
    angle = phase.astype(np.float32) * np.float32(2.0 * math.pi / samples)
    factor = np.float32(1.0 / math.sqrt(samples))
    cosine, sine = np.cos(angle) * factor, -np.sin(angle) * factor
    step = np.arange(samples)
    size = np.where(step % 2 == 0, factor, np.cos(np.float32(math.pi / 4)) * factor)
    sine[0] = np.where(step // 4 % 2 == 0, size, -size)
    rows = np.concatenate([cosine, sine]).reshape(2 * quarter, samples // 4, 4)
    return rows.transpose(2, 0, 1).astype(jnp.bfloat16)


def mirror(quarter):
    places = (quarter - np.arange(quarter)) % quarter
    return np.eye(quarter, dtype=np.float32)[places].astype(jnp.bfloat16)


def halves(x):
    high = x.astype(jnp.bfloat16)
    return high, (x - high.astype(jnp.float32)).astype(jnp.bfloat16)


def exchange_groups(spaces, bands):
    space_bits, band_bits = spaces.bit_length() - 1, bands.bit_length() - 1
    bits = list(range(space_bits + band_bits))
    first = [bit for bit in (0, space_bits) if bit in bits and (bit == 0 or band_bits)]
    first = sorted(set(first))
    return [first] + [[bit] for bit in bits if bit not in first]


def place_of(delta, groups):
    order = [bit for group in groups for bit in group]
    place = 0
    for k, bit in enumerate(order):
        place = place | (((delta >> bit) & 1) << (len(order) - 1 - k))
    crossings = 0
    for group in groups:
        met = 0
        for bit in group:
            met = met | ((delta >> bit) & 1)
        crossings = crossings ^ met
    return place, crossings


def source_kernel(
    sizes,
    table_ref,
    low_ref,
    high_ref,
    mirror_ref,
    seismic_hbm,
    rows_hbm,
    leaf_hbm,
    moves_hbm,
    keep_ref,
    send_ref,
    seismic_ref,
    wide_ref,
    rows_ref,
    leaf_ref,
    moves_ref,
    spectra_ref,
    now_ref,
    next_ref,
    sems,
):
    traces, samples, shots, freq_total, rank, bands, spaces, subs = sizes
    quarter = freq_total // 4
    freq_block = freq_total // bands
    boxes = bands * spaces
    box_bits = boxes.bit_length() - 1
    space_bits = spaces.bit_length() - 1
    part = rank // subs
    groups = exchange_groups(spaces, bands)
    own_space, own_sub = lax.axis_index("space"), lax.axis_index("sub")
    own_box = lax.axis_index("trace") * spaces + own_space

    copies = []
    for source, target in (
        [(rows_hbm, rows_ref)]
        + [(seismic_hbm.at[j], seismic_ref.at[j]) for j in range(traces)]
        + [(leaf_hbm, leaf_ref), (moves_hbm, moves_ref)]
    ):
        copy = pltpu.make_async_copy(source, target, sems.at[len(copies)])
        copy.start()
        copies.append(copy)

    row = lax.broadcasted_iota(jnp.int32, (quarter, shots), 0)
    mirrored = jnp.where(row == 0, 0, quarter - row)
    kept = []
    for q in range(4):
        freq = q * quarter + (mirrored if q % 2 else row)
        kept.append((freq >= low_ref[...]) & (freq < high_ref[...]))
    top = lax.broadcasted_iota(jnp.int32, (8, 2 * shots), 0) == 0

    copies[0].wait()
    for j in range(0, traces, 2):
        for k in range(2):
            copies[1 + j + k].wait()
            wide_ref[j + k] = seismic_ref[j + k].astype(jnp.float32)
        sums = []
        for r in range(4):
            pair = jnp.concatenate(
                [wide_ref[j + k, pl.ds(r, samples // 4, stride=4), :].astype(jnp.bfloat16) for k in range(2)], axis=1
            )
            sums.append(jnp.dot(rows_ref[r], pair, preferred_element_type=jnp.float32))
        for start in range(0, quarter, 8):
            cos = [x[start : start + 8] for x in sums]
            sin = [x[quarter + start : quarter + start + 8] for x in sums]
            extra = sin
            if start == 0:
                sin = [jnp.where(top, 0.0, x) for x in sin]
            even, odd, even_gap, odd_gap = cos[0] + cos[2], cos[1] + cos[3], cos[0] - cos[2], cos[3] - cos[1]
            s_even, s_odd, s_even_gap, s_odd_gap = sin[0] + sin[2], sin[1] + sin[3], sin[0] - sin[2], sin[1] - sin[3]
            real = [even + odd, even_gap - s_odd_gap, even_gap + s_odd_gap, even - odd]
            imag = [s_even + s_odd, odd_gap - s_even_gap, odd_gap + s_even_gap, s_odd - s_even]
            if start == 0:
                gap, both = extra[1] - extra[3], extra[1] + extra[3]
                real[1] = jnp.where(top, extra[0] + gap, real[1])
                imag[1] = jnp.where(top, -extra[2] - both, imag[1])
                real[3] = jnp.where(top, extra[0] - gap, real[3])
                imag[3] = jnp.where(top, extra[2] - both, imag[3])
            for q in range(4):
                keep = kept[q][start : start + 8]
                for k in range(2):
                    for c, piece in enumerate((real[q], imag[q])):
                        piece = jnp.where(keep, piece[:, k * shots : (k + 1) * shots], 0.0)
                        spectra_ref[q, pl.ds((j + k) * quarter + start, 8), pl.ds(c * shots, shots)] = piece.astype(jnp.bfloat16)
    copies[traces + 1].wait()
    for q in range(4):
        blocks = jnp.concatenate([leaf_ref[j, :, pl.ds(q * quarter, quarter)] for j in range(traces)], axis=0)
        if q % 2:
            blocks = jnp.dot(blocks, mirror_ref[...], preferred_element_type=jnp.float32).astype(jnp.bfloat16)
        left = jnp.concatenate([blocks[j * 2 * rank : (j + 1) * 2 * rank] for j in range(traces)], axis=1)
        for g in range(q * quarter // freq_block, -(-(q + 1) * quarter // freq_block)):
            own = left
            if freq_block < quarter:
                lane = lax.broadcasted_iota(jnp.int32, left.shape, 1) % quarter
                freq = q * quarter + (jnp.where(lane == 0, 0, quarter - lane) if q % 2 else lane)
                own = jnp.where(freq // freq_block == g, left, jnp.zeros_like(left))
            total = jnp.dot(own, spectra_ref[q], preferred_element_type=jnp.float32)
            parts = [total[:rank, :shots] - total[rank:, shots:], total[rank:, :shots] + total[:rank, shots:]]
            if q * quarter > g * freq_block:
                parts = [now_ref[g, :rank] + parts[0], now_ref[g, rank:] + parts[1]]
            now_ref[g, :rank], now_ref[g, rank:] = parts
    copies[traces + 2].wait()

    def complex_rows(entry):
        real, imag = moves_ref[entry, 0], moves_ref[entry, 1]
        return jnp.concatenate(
            [jnp.concatenate([real, -imag], axis=1), jnp.concatenate([imag, real], axis=1)], axis=0
        )

    def level(section_no, source, store):
        stride = 1 << section_no
        inside = section_no < space_bits
        count = boxes // 2 if not inside else bands * (1 << section_no)

        def body(i, carry):
            if inside:
                done = i % stride
                band = i // stride
                above = (own_space >> (section_no + 1)) << (section_no + 1)
                lower = band * spaces + above + done
                own_bit = (own_space >> section_no) & 1
                right = source[i]
                mats = [
                    complex_rows(table_ref[section_no, own_bit, lower + upper * stride])
                    for upper in range(2)
                ]
                places = [band * (2 * stride) + upper * stride + done for upper in range(2)]
            else:
                lower = (i // stride) * (2 * stride) + i % stride
                right = jnp.concatenate([source[lower], source[lower + stride]], axis=0)
                mats = [
                    jnp.concatenate(
                        [
                            complex_rows(table_ref[section_no, child, lower + upper * stride])
                            for child in range(2)
                        ],
                        axis=1,
                    )
                    for upper in range(2)
                ]
                places = [lower, lower + stride]
            left_high, left_low = halves(jnp.concatenate(mats, axis=0))
            right_high, right_low = halves(right)
            left = jnp.concatenate([left_high, left_low], axis=0)
            wide = jnp.concatenate([right_high, right_low], axis=1)
            product = jnp.dot(left, wide, preferred_element_type=jnp.float32)
            product = product[:, :shots] + product[:, shots:]
            product = product[: 4 * rank] + product[4 * rank :]
            for upper in range(2):
                store(places[upper], product[upper * 2 * rank : (upper + 1) * 2 * rank])
            return carry

        lax.fori_loop(0, count, body, 0, unroll=count <= 4)

    def store_last(box, value):
        place, crossings = place_of(box ^ own_box, groups)
        first, second = (
            jnp.stack([value[half * part : (half + 1) * part], value[rank + half * part : rank + (half + 1) * part]])
            for half in range(2)
        )
        keep_first = (own_sub ^ crossings) == 0
        keep_ref[place] = jnp.where(keep_first, first, second)
        send_ref[place] = jnp.where(keep_first, second, first).astype(jnp.bfloat16)

    def store_in(ref):
        def store(box, value):
            ref[box] = value

        return store

    sources = [now_ref, next_ref]
    for section_no in range(box_bits):
        last = section_no == box_bits - 1
        level(section_no, sources[section_no % 2], store_last if last else store_in(sources[(section_no + 1) % 2]))


def per_device(seismic, band_low, band_high, leaf_weights, translations, level_table):
    bands, spaces, subs = (lax.axis_size(name) for name in ("trace", "space", "sub"))
    traces, samples, shots = seismic.shape
    freq_total, rank = leaf_weights.shape[1], leaf_weights.shape[3]
    boxes = bands * spaces
    rows = jnp.asarray(spectral_rows(freq_total, samples))
    leaf = leaf_weights.transpose(0, 2, 3, 1).reshape(traces, 2 * rank, freq_total)
    tail = (2, rank // subs, shots)
    kind = pltpu.VMEM if boxes * 2 * rank * shots <= 1 << 18 else jax.ShapeDtypeStruct
    smem = pl.BlockSpec(memory_space=pltpu.SMEM)
    vmem = pl.BlockSpec(memory_space=pltpu.VMEM)
    anywhere = pl.BlockSpec(memory_space=pl.ANY)
    keep, send = pl.pallas_call(
        functools.partial(source_kernel, (traces, samples, shots, freq_total, rank, bands, spaces, subs)),
        out_shape=(
            kind((boxes,) + tail, jnp.float32),
            kind((boxes,) + tail, jnp.bfloat16),
        ),
        in_specs=[smem, vmem, vmem, vmem] + [anywhere] * 4,
        out_specs=(vmem, vmem),
        scratch_shapes=[
            pltpu.VMEM(seismic.shape, jnp.bfloat16),
            pltpu.VMEM(seismic.shape, jnp.float32),
            pltpu.VMEM(rows.shape, jnp.bfloat16),
            pltpu.VMEM(leaf.shape, jnp.bfloat16),
            pltpu.VMEM(translations.shape, jnp.float32),
            pltpu.VMEM((4, traces * freq_total // 4, 2 * shots), jnp.bfloat16),
            pltpu.VMEM((boxes, 2 * rank, shots), jnp.float32),
            pltpu.VMEM((boxes, 2 * rank, shots), jnp.float32),
            pltpu.SemaphoreType.DMA((traces + 3,)),
        ],
        name="source",
    )(
        level_table.transpose(0, 2, 1),
        band_low[None, :],
        band_high[None, :],
        jnp.asarray(mirror(freq_total // 4)),
        seismic,
        rows,
        leaf,
        translations,
    )

    axes = ("trace", "space", "sub")

    def swapped(x, mask, flip):
        return lax.ppermute(x, axes, [(i, ((i >> 1 ^ mask) << 1) | (i & 1 ^ flip)) for i in range(2 * boxes)])

    total = keep + swapped(send, 0, 1).astype(jnp.float32)
    for group in exchange_groups(spaces, bands):
        count = 1 << len(group)
        shares = total.reshape((count, -1) + tail)
        total = shares[0]
        for share in range(count - 1, 0, -1):
            mask = sum(1 << bit for k, bit in enumerate(group) if share >> (len(group) - 1 - k) & 1)
            total = total + swapped(shares[share].astype(jnp.bfloat16), mask, 1).astype(jnp.float32)
    return total


def solution(mesh):
    placed = (
        P(("groups", "trace", "space", "sub"), None, None),
        P("groups"),
        P("groups"),
        P(),
        P(),
        P(),
    )
    return jax.shard_map(
        per_device,
        mesh=mesh,
        in_specs=placed,
        out_specs=P(("groups", "trace", "space"), None, "sub", None),
        check_vma=False,
    )
```

```python
import functools
import math

import jax
import jax.numpy as jnp
import numpy as np
from jax import lax
from jax.experimental import pallas as pl
from jax.experimental.pallas import tpu as pltpu
from jax.sharding import PartitionSpec as P

SLAB = 8

def spectral_rows(freq_total, samples):
    quarter = freq_total // 4
    phase = (np.arange(quarter)[:, None] * np.arange(samples)[None, :]) % samples
    angle = phase.astype(np.float32) * np.float32(2.0 * math.pi / samples)
    factor = np.float32(1.0 / math.sqrt(samples))
    cosine, sine = np.cos(angle) * factor, -np.sin(angle) * factor
    step = np.arange(samples)
    size = np.where(step % 2 == 0, factor, np.cos(np.float32(math.pi / 4)) * factor)
    sine[0] = np.where(step // 4 % 2 == 0, size, -size)
    rows = np.concatenate([cosine, sine]).reshape(2 * quarter, samples // 4, 4)
    return rows.transpose(2, 0, 1).astype(jnp.bfloat16)


def halves(x):
    high = x.astype(jnp.bfloat16)
    return high, (x - high.astype(jnp.float32)).astype(jnp.bfloat16)


def exchange_groups(spaces, bands):
    space_bits, band_bits = spaces.bit_length() - 1, bands.bit_length() - 1
    bits = list(range(space_bits + band_bits))
    first = [bit for bit in (0, space_bits) if bit in bits and (bit == 0 or band_bits)]
    first = sorted(set(first))
    return [first] + [[bit] for bit in bits if bit not in first]


def place_of(delta, groups):
    order = [bit for group in groups for bit in group]
    place = 0
    for k, bit in enumerate(order):
        place = place | (((delta >> bit) & 1) << (len(order) - 1 - k))
    crossings = 0
    for group in groups:
        met = 0
        for bit in group:
            met = met | ((delta >> bit) & 1)
        crossings = crossings ^ met
    return place, crossings


def source_kernel(
    sizes,
    table_hbm,
    low_hbm,
    high_hbm,
    seismic_hbm,
    rows_hbm,
    leaf_hbm,
    moves_hbm,
    keep_ref,
    send_ref,
    table_ref,
    low_ref,
    high_ref,
    seismic_ref,
    wide_ref,
    rows_ref,
    leaf_ref,
    moves_ref,
    spectra_ref,
    first_high_ref,
    first_low_ref,
    second_high_ref,
    second_low_ref,
    sems,
):
    traces, samples, shots, freq_total, rank, bands, spaces, subs = sizes
    quarter = freq_total // 4
    freq_block = freq_total // bands
    boxes = bands * spaces
    box_bits = boxes.bit_length() - 1
    space_bits = spaces.bit_length() - 1
    part = rank // subs
    groups = exchange_groups(spaces, bands)
    own_space, own_sub = lax.axis_index("space"), lax.axis_index("sub")
    own_box = lax.axis_index("trace") * spaces + own_space

    copies = []
    for source, target in (
        [(low_hbm, low_ref), (high_hbm, high_ref), (rows_hbm, rows_ref)]
        + [(seismic_hbm.at[j], seismic_ref.at[j]) for j in range(traces)]
        + [(leaf_hbm, leaf_ref), (moves_hbm, moves_ref), (table_hbm, table_ref)]
    ):
        copy = pltpu.make_async_copy(source, target, sems.at[len(copies)])
        copy.start()
        copies.append(copy)
    low_copy, high_copy, rows_copy = copies[:3]
    trace_copies, (leaf_copy, moves_copy, table_copy) = copies[3 : 3 + traces], copies[3 + traces :]

    low_copy.wait()
    high_copy.wait()
    row = lax.broadcasted_iota(jnp.int32, (quarter, shots), 0)
    mirrored = jnp.where(row == 0, 0, quarter - row)
    kept = []
    for q in range(4):
        freq = q * quarter + (mirrored if q % 2 else row)
        kept.append((freq >= low_ref[...]) & (freq < high_ref[...]))
    top = lax.broadcasted_iota(jnp.int32, (SLAB, 2 * shots), 0) == 0

    rows_copy.wait()
    for j in range(0, traces, 2):
        for k in range(2):
            trace_copies[j + k].wait()
            wide_ref[j + k] = seismic_ref[j + k].astype(jnp.float32)
        sums = []
        for r in range(4):
            pair = jnp.concatenate(
                [wide_ref[j + k, pl.ds(r, samples // 4, stride=4), :].astype(jnp.bfloat16) for k in range(2)], axis=1
            )
            sums.append(jnp.dot(rows_ref[r], pair, preferred_element_type=jnp.float32))
        for start in range(0, quarter, SLAB):
            cos = [x[start : start + SLAB] for x in sums]
            sin = [x[quarter + start : quarter + start + SLAB] for x in sums]
            extra = sin
            if start == 0:
                sin = [jnp.where(top, 0.0, x) for x in sin]
            even, odd, even_gap, odd_gap = cos[0] + cos[2], cos[1] + cos[3], cos[0] - cos[2], cos[3] - cos[1]
            s_even, s_odd, s_even_gap, s_odd_gap = sin[0] + sin[2], sin[1] + sin[3], sin[0] - sin[2], sin[1] - sin[3]
            real = [even + odd, even_gap - s_odd_gap, even_gap + s_odd_gap, even - odd]
            imag = [s_even + s_odd, odd_gap - s_even_gap, odd_gap + s_even_gap, s_odd - s_even]
            if start == 0:
                gap, both = extra[1] - extra[3], extra[1] + extra[3]
                real[1] = jnp.where(top, extra[0] + gap, real[1])
                imag[1] = jnp.where(top, -extra[2] - both, imag[1])
                real[3] = jnp.where(top, extra[0] - gap, real[3])
                imag[3] = jnp.where(top, extra[2] - both, imag[3])
            for q in range(4):
                keep = kept[q][start : start + SLAB]
                for c, piece in enumerate((real[q], imag[q])):
                    for k in range(2):
                        spectra_ref[q, pl.ds((j + k) * quarter + start, SLAB), pl.ds(c * shots, shots)] = jnp.where(
                            keep, piece[:, k * shots : (k + 1) * shots], 0.0
                        ).astype(jnp.bfloat16)

    leaf_copy.wait()
    flip = lax.broadcasted_iota(jnp.int32, (quarter, quarter), 0) + lax.broadcasted_iota(jnp.int32, (quarter, quarter), 1)
    flip = jnp.where((flip == 0) | (flip == quarter), 1.0, 0.0).astype(jnp.bfloat16)
    totals = [None] * bands
    for q in range(4):
        blocks = jnp.concatenate([leaf_ref[j, :, pl.ds(q * quarter, quarter)] for j in range(traces)], axis=0)
        if q % 2:
            blocks = jnp.dot(blocks, flip, preferred_element_type=jnp.float32).astype(jnp.bfloat16)
        left = jnp.concatenate([blocks[j * 2 * rank : (j + 1) * 2 * rank] for j in range(traces)], axis=1)
        for g in range(q * quarter // freq_block, -(-(q + 1) * quarter // freq_block)):
            own = left
            if freq_block < quarter:
                lane = lax.broadcasted_iota(jnp.int32, left.shape, 1) % quarter
                freq = q * quarter + (jnp.where(lane == 0, 0, quarter - lane) if q % 2 else lane)
                own = jnp.where(freq // freq_block == g, left, jnp.zeros_like(left))
            total = jnp.dot(own, spectra_ref[q], preferred_element_type=jnp.float32)
            totals[g] = total if totals[g] is None else totals[g] + total

    def joined(product):
        real = product[:rank, :shots] - product[rank:, shots:]
        imag = product[rank:, :shots] + product[:rank, shots:]
        return jnp.concatenate([real, imag], axis=1)

    def store_in(refs):
        def store(box, value):
            refs[0][box], refs[1][box] = halves(value)

        return store

    def store_last(box, value):
        place, crossings = place_of(box ^ own_box, groups)
        first, second = (
            jnp.stack([value[half * part : (half + 1) * part, c * shots : (c + 1) * shots] for c in range(2)])
            for half in range(2)
        )
        keep_first = (own_sub ^ crossings) == 0
        keep_ref[place] = jnp.where(keep_first, first, second)
        send_ref[place] = jnp.where(keep_first, second, first).astype(jnp.bfloat16)

    held = [(first_high_ref, first_low_ref), (second_high_ref, second_low_ref)]
    for g in range(bands):
        store_in(held[0])(g, joined(totals[g]))
    moves_copy.wait()
    table_copy.wait()

    def level(section_no, source, store):
        stride = 1 << section_no
        inside = section_no < space_bits
        count = bands * stride if inside else boxes // 2
        high_ref, low_ref = source

        def pair(i):
            if inside:
                done, band = i % stride, i // stride
                lower = band * spaces + ((own_space >> (section_no + 1)) << (section_no + 1)) + done
                own_bit = (own_space >> section_no) & 1
                children, held_at = [own_bit, own_bit], [i]
                places = [band * (2 * stride) + upper * stride + done for upper in range(2)]
            else:
                lower = (i // stride) * (2 * stride) + i % stride
                children, held_at = [0, 1], [lower, lower + stride]
                places = [lower, lower + stride]
            entries = [[table_ref[section_no, child, lower + upper * stride] for child in children] for upper in range(2)]
            left = jnp.concatenate(
                [
                    jnp.concatenate([moves_ref[entry, c] for entry in entries[upper]], axis=1)
                    for upper in range(2)
                    for c in range(2)
                ],
                axis=0,
            )
            high = left.astype(jnp.bfloat16)
            rest = left - high.astype(jnp.float32)
            right_high = [high_ref[k] for k in held_at]
            right_low = [low_ref[k] for k in held_at]
            if inside:
                lane = lax.broadcasted_iota(jnp.int32, left.shape, 1)
                left = [jnp.where(lane < rank, high.astype(jnp.float32), rest).astype(jnp.bfloat16), high]
                right = right_high * 2 + right_low + [jnp.zeros_like(right_low[0])]
            else:
                left = [high, rest.astype(jnp.bfloat16), high]
                right = right_high * 2 + right_low
            product = jnp.dot(
                jnp.concatenate(left, axis=1), jnp.concatenate(right, axis=0), preferred_element_type=jnp.float32
            )
            for upper in range(2):
                store(places[upper], joined(product[upper * 2 * rank : (upper + 1) * 2 * rank]))

        if count <= 4:
            for i in range(count):
                pair(i)
        else:
            lax.fori_loop(0, count, lambda i, carry: (pair(i), carry)[1], 0)

    for section_no in range(box_bits):
        last = section_no == box_bits - 1
        level(section_no, held[section_no % 2], store_last if last else store_in(held[(section_no + 1) % 2]))


def per_device(seismic, band_low, band_high, leaf_weights, translations, level_table):
    bands, spaces, subs = (lax.axis_size(name) for name in ("trace", "space", "sub"))
    traces, samples, shots = seismic.shape
    freq_total, rank = leaf_weights.shape[1], leaf_weights.shape[3]
    boxes = bands * spaces
    rows = jnp.asarray(spectral_rows(freq_total, samples))
    leaf = leaf_weights.transpose(0, 2, 3, 1).reshape(traces, 2 * rank, freq_total)
    tail = (2, rank // subs, shots)
    kind = pltpu.VMEM if boxes * 2 * rank * shots <= 1 << 18 else jax.ShapeDtypeStruct
    vmem = pl.BlockSpec(memory_space=pltpu.VMEM)
    anywhere = pl.BlockSpec(memory_space=pl.ANY)
    keep, send = pl.pallas_call(
        functools.partial(source_kernel, (traces, samples, shots, freq_total, rank, bands, spaces, subs)),
        out_shape=(
            kind((boxes,) + tail, jnp.float32),
            kind((boxes,) + tail, jnp.bfloat16),
        ),
        in_specs=[anywhere] * 7,
        out_specs=(vmem, vmem),
        scratch_shapes=[
            pltpu.SMEM((level_table.shape[0], 2, boxes), jnp.int32),
            pltpu.VMEM((1, shots), jnp.int32),
            pltpu.VMEM((1, shots), jnp.int32),
            pltpu.VMEM(seismic.shape, jnp.bfloat16),
            pltpu.VMEM(seismic.shape, jnp.float32),
            pltpu.VMEM(rows.shape, jnp.bfloat16),
            pltpu.VMEM(leaf.shape, jnp.bfloat16),
            pltpu.VMEM(translations.shape, jnp.float32),
            pltpu.VMEM((4, traces * freq_total // 4, 2 * shots), jnp.bfloat16),
        ]
        + [pltpu.VMEM((boxes, rank, 2 * shots), jnp.bfloat16)] * 4
        + [pltpu.SemaphoreType.DMA((traces + 6,))],
        name="source",
    )(
        level_table.transpose(0, 2, 1),
        band_low[None, :],
        band_high[None, :],
        seismic,
        rows,
        leaf,
        translations,
    )

    axes = ("trace", "space", "sub")

    def swapped(x, mask, flip):
        return lax.ppermute(x, axes, [(i, ((i >> 1 ^ mask) << 1) | (i & 1 ^ flip)) for i in range(2 * boxes)])

    total = keep + swapped(send, 0, 1).astype(jnp.float32)
    for group in exchange_groups(spaces, bands):
        count = 1 << len(group)
        shares = total.reshape((count, -1) + tail)
        total = shares[0]
        for share in range(count - 1, 0, -1):
            mask = sum(1 << bit for k, bit in enumerate(group) if share >> (len(group) - 1 - k) & 1)
            total = total + swapped(shares[share].astype(jnp.bfloat16), mask, 1).astype(jnp.float32)
    return total


def solution(mesh):
    placed = (
        P(("groups", "trace", "space", "sub"), None, None),
        P("groups"),
        P("groups"),
        P(),
        P(),
        P(),
    )
    return jax.shard_map(
        per_device,
        mesh=mesh,
        in_specs=placed,
        out_specs=P(("groups", "trace", "space"), None, "sub", None),
        check_vma=False,
    )
```

```python
import functools
import math

import jax
import jax.numpy as jnp
import numpy as np
from jax import lax
from jax.experimental import pallas as pl
from jax.experimental.pallas import tpu as pltpu
from jax.sharding import PartitionSpec as P

SLAB = 8

def spectral_rows(freq_total, samples):
    quarter = freq_total // 4
    phase = (np.arange(quarter)[:, None] * np.arange(samples)[None, :]) % samples
    angle = phase.astype(np.float32) * np.float32(2.0 * math.pi / samples)
    factor = np.float32(1.0 / math.sqrt(samples))
    cosine, sine = np.cos(angle) * factor, -np.sin(angle) * factor
    step = np.arange(samples)
    size = np.where(step % 2 == 0, factor, np.cos(np.float32(math.pi / 4)) * factor)
    sine[0] = np.where(step // 4 % 2 == 0, size, -size)
    rows = np.concatenate([cosine, sine]).reshape(2 * quarter, samples // 4, 4)
    return rows.transpose(2, 0, 1).astype(jnp.bfloat16)


def halves(x):
    high = x.astype(jnp.bfloat16)
    return high, (x - high.astype(jnp.float32)).astype(jnp.bfloat16)


def exchange_groups(spaces, bands):
    space_bits, band_bits = spaces.bit_length() - 1, bands.bit_length() - 1
    bits = list(range(space_bits + band_bits))
    first = [bit for bit in (0, space_bits) if bit in bits and (bit == 0 or band_bits)]
    first = sorted(set(first))
    return [first] + [[bit] for bit in bits if bit not in first]


def place_of(delta, groups):
    order = [bit for group in groups for bit in group]
    place = 0
    for k, bit in enumerate(order):
        place = place | (((delta >> bit) & 1) << (len(order) - 1 - k))
    crossings = 0
    for group in groups:
        met = 0
        for bit in group:
            met = met | ((delta >> bit) & 1)
        crossings = crossings ^ met
    return place, crossings


def source_kernel(
    sizes,
    table_hbm,
    low_hbm,
    high_hbm,
    seismic_hbm,
    rows_hbm,
    leaf_hbm,
    moves_hbm,
    keep_ref,
    send_ref,
    table_ref,
    low_ref,
    high_ref,
    seismic_ref,
    wide_ref,
    rows_ref,
    leaf_ref,
    moves_ref,
    spectra_ref,
    first_high_ref,
    first_low_ref,
    second_high_ref,
    second_low_ref,
    sems,
):
    traces, samples, shots, freq_total, rank, bands, spaces, subs = sizes
    quarter = freq_total // 4
    freq_block = freq_total // bands
    boxes = bands * spaces
    box_bits = boxes.bit_length() - 1
    space_bits = spaces.bit_length() - 1
    part = rank // subs
    groups = exchange_groups(spaces, bands)
    own_space, own_sub = lax.axis_index("space"), lax.axis_index("sub")
    own_box = lax.axis_index("trace") * spaces + own_space

    copies = []
    for source, target in (
        [(low_hbm, low_ref), (high_hbm, high_ref)]
        + [(seismic_hbm.at[j], seismic_ref.at[j]) for j in range(2)]
        + [(rows_hbm, rows_ref)]
        + [(seismic_hbm.at[j], seismic_ref.at[j]) for j in range(2, traces)]
        + [(leaf_hbm, leaf_ref), (moves_hbm, moves_ref), (table_hbm, table_ref)]
    ):
        copy = pltpu.make_async_copy(source, target, sems.at[len(copies)])
        copy.start()
        copies.append(copy)
    low_copy, high_copy, rows_copy = copies[0], copies[1], copies[4]
    trace_copies, (leaf_copy, moves_copy, table_copy) = copies[2:4] + copies[5 : 3 + traces], copies[3 + traces :]

    low_copy.wait()
    high_copy.wait()
    row = lax.broadcasted_iota(jnp.int32, (quarter, shots), 0)
    mirrored = jnp.where(row == 0, 0, quarter - row)
    kept = []
    for q in range(4):
        freq = q * quarter + (mirrored if q % 2 else row)
        kept.append((freq >= low_ref[...]) & (freq < high_ref[...]))
    top = lax.broadcasted_iota(jnp.int32, (SLAB, 2 * shots), 0) == 0

    for j in range(0, traces, 2):
        for k in range(2):
            trace_copies[j + k].wait()
            wide_ref[j + k] = seismic_ref[j + k].astype(jnp.float32)
        if j == 0:
            rows_copy.wait()
        sums = []
        for r in range(4):
            pair = jnp.concatenate(
                [wide_ref[j + k, pl.ds(r, samples // 4, stride=4), :].astype(jnp.bfloat16) for k in range(2)], axis=1
            )
            sums.append(jnp.dot(rows_ref[r], pair, preferred_element_type=jnp.float32))
        for start in range(0, quarter, SLAB):
            cos = [x[start : start + SLAB] for x in sums]
            sin = [x[quarter + start : quarter + start + SLAB] for x in sums]
            extra = sin
            if start == 0:
                sin = [jnp.where(top, 0.0, x) for x in sin]
            even, odd, even_gap, odd_gap = cos[0] + cos[2], cos[1] + cos[3], cos[0] - cos[2], cos[3] - cos[1]
            s_even, s_odd, s_even_gap, s_odd_gap = sin[0] + sin[2], sin[1] + sin[3], sin[0] - sin[2], sin[1] - sin[3]
            real = [even + odd, even_gap - s_odd_gap, even_gap + s_odd_gap, even - odd]
            imag = [s_even + s_odd, odd_gap - s_even_gap, odd_gap + s_even_gap, s_odd - s_even]
            if start == 0:
                gap, both = extra[1] - extra[3], extra[1] + extra[3]
                real[1] = jnp.where(top, extra[0] + gap, real[1])
                imag[1] = jnp.where(top, -extra[2] - both, imag[1])
                real[3] = jnp.where(top, extra[0] - gap, real[3])
                imag[3] = jnp.where(top, extra[2] - both, imag[3])
            for q in range(4):
                keep = kept[q][start : start + SLAB]
                for c, piece in enumerate((real[q], imag[q])):
                    for k in range(2):
                        spectra_ref[q, pl.ds((j + k) * quarter + start, SLAB), pl.ds(c * shots, shots)] = jnp.where(
                            keep, piece[:, k * shots : (k + 1) * shots], 0.0
                        ).astype(jnp.bfloat16)

    leaf_copy.wait()
    moves_copy.wait()
    table_copy.wait()
    lane = lax.broadcasted_iota(jnp.int32, (2 * rank, quarter), 1)
    flip = jnp.where(lane == 0, 0, quarter - lane)
    totals = [None] * bands
    for q in range(4):
        blocks = [leaf_ref[j, :, pl.ds(q * quarter, quarter)] for j in range(traces)]
        if q % 2:
            blocks = [jnp.take_along_axis(x.astype(jnp.float32), flip, axis=1).astype(jnp.bfloat16) for x in blocks]
        left = jnp.concatenate(blocks, axis=1)
        for g in range(q * quarter // freq_block, -(-(q + 1) * quarter // freq_block)):
            own = left
            if freq_block < quarter:
                lane = lax.broadcasted_iota(jnp.int32, left.shape, 1) % quarter
                freq = q * quarter + (jnp.where(lane == 0, 0, quarter - lane) if q % 2 else lane)
                own = jnp.where(freq // freq_block == g, left, jnp.zeros_like(left))
            total = jnp.dot(own, spectra_ref[q], preferred_element_type=jnp.float32)
            totals[g] = total if totals[g] is None else totals[g] + total

    def joined(product):
        real = product[:rank, :shots] - product[rank:, shots:]
        imag = product[rank:, :shots] + product[:rank, shots:]
        return jnp.concatenate([real, imag], axis=1)

    def store_in(refs):
        def store(box, value):
            refs[0][box], refs[1][box] = halves(value)

        return store

    def store_last(box, value):
        place, crossings = place_of(box ^ own_box, groups)
        first, second = (
            jnp.stack([value[half * part : (half + 1) * part, c * shots : (c + 1) * shots] for c in range(2)])
            for half in range(2)
        )
        keep_first = (own_sub ^ crossings) == 0
        keep_ref[place] = jnp.where(keep_first, first, second)
        send_ref[place] = jnp.where(keep_first, second, first).astype(jnp.bfloat16)

    held = [(first_high_ref, first_low_ref), (second_high_ref, second_low_ref)]
    for g in range(bands):
        store_in(held[0])(g, joined(totals[g]))

    def level(section_no, source, store):
        stride = 1 << section_no
        inside = section_no < space_bits
        count = bands * stride if inside else boxes // 2
        high_ref, low_ref = source

        def pair(i):
            if inside:
                done, band = i % stride, i // stride
                lower = band * spaces + ((own_space >> (section_no + 1)) << (section_no + 1)) + done
                own_bit = (own_space >> section_no) & 1
                children, held_at = [own_bit, own_bit], [i]
                places = [band * (2 * stride) + upper * stride + done for upper in range(2)]
            else:
                lower = (i // stride) * (2 * stride) + i % stride
                children, held_at = [0, 1], [lower, lower + stride]
                places = [lower, lower + stride]
            entries = [[table_ref[section_no, child, lower + upper * stride] for child in children] for upper in range(2)]
            left = jnp.concatenate(
                [
                    jnp.concatenate([moves_ref[entry, c] for entry in entries[upper]], axis=1)
                    for upper in range(2)
                    for c in range(2)
                ],
                axis=0,
            )
            high = left.astype(jnp.bfloat16)
            rest = left - high.astype(jnp.float32)
            right_high = [high_ref[k] for k in held_at]
            right_low = [low_ref[k] for k in held_at]
            if inside:
                lane = lax.broadcasted_iota(jnp.int32, left.shape, 1)
                left = [jnp.where(lane < rank, high.astype(jnp.float32), rest).astype(jnp.bfloat16), high]
                right = right_high * 2 + right_low + [jnp.zeros_like(right_low[0])]
            else:
                left = [high, rest.astype(jnp.bfloat16), high]
                right = right_high * 2 + right_low
            product = jnp.dot(
                jnp.concatenate(left, axis=1), jnp.concatenate(right, axis=0), preferred_element_type=jnp.float32
            )
            for upper in range(2):
                store(places[upper], joined(product[upper * 2 * rank : (upper + 1) * 2 * rank]))

        if count <= 4:
            for i in range(count):
                pair(i)
        else:
            lax.fori_loop(0, count, lambda i, carry: (pair(i), carry)[1], 0)

    for section_no in range(box_bits):
        last = section_no == box_bits - 1
        level(section_no, held[section_no % 2], store_last if last else store_in(held[(section_no + 1) % 2]))


def per_device(seismic, band_low, band_high, leaf_weights, translations, level_table):
    bands, spaces, subs = (lax.axis_size(name) for name in ("trace", "space", "sub"))
    traces, samples, shots = seismic.shape
    freq_total, rank = leaf_weights.shape[1], leaf_weights.shape[3]
    boxes = bands * spaces
    rows = jnp.asarray(spectral_rows(freq_total, samples))
    leaf = leaf_weights.transpose(0, 2, 3, 1).reshape(traces, 2 * rank, freq_total)
    tail = (2, rank // subs, shots)
    kind = pltpu.VMEM if boxes * 2 * rank * shots <= 1 << 18 else jax.ShapeDtypeStruct
    vmem = pl.BlockSpec(memory_space=pltpu.VMEM)
    anywhere = pl.BlockSpec(memory_space=pl.ANY)
    keep, send = pl.pallas_call(
        functools.partial(source_kernel, (traces, samples, shots, freq_total, rank, bands, spaces, subs)),
        out_shape=(
            kind((boxes,) + tail, jnp.float32),
            kind((boxes,) + tail, jnp.bfloat16),
        ),
        in_specs=[anywhere] * 7,
        out_specs=(vmem, vmem),
        scratch_shapes=[
            pltpu.SMEM((level_table.shape[0], 2, boxes), jnp.int32),
            pltpu.VMEM((1, shots), jnp.int32),
            pltpu.VMEM((1, shots), jnp.int32),
            pltpu.VMEM(seismic.shape, jnp.bfloat16),
            pltpu.VMEM(seismic.shape, jnp.float32),
            pltpu.VMEM(rows.shape, jnp.bfloat16),
            pltpu.VMEM(leaf.shape, jnp.bfloat16),
            pltpu.VMEM(translations.shape, jnp.float32),
            pltpu.VMEM((4, traces * freq_total // 4, 2 * shots), jnp.bfloat16),
        ]
        + [pltpu.VMEM((boxes, rank, 2 * shots), jnp.bfloat16)] * 4
        + [pltpu.SemaphoreType.DMA((traces + 6,))],
        name="source",
    )(
        level_table.transpose(0, 2, 1),
        band_low[None, :],
        band_high[None, :],
        seismic,
        rows,
        leaf,
        translations,
    )

    axes = ("trace", "space", "sub")

    def swapped(x, mask, flip):
        return lax.ppermute(x, axes, [(i, ((i >> 1 ^ mask) << 1) | (i & 1 ^ flip)) for i in range(2 * boxes)])

    total = keep + swapped(send, 0, 1).astype(jnp.float32)
    for group in exchange_groups(spaces, bands):
        count = 1 << len(group)
        shares = total.reshape((count, -1) + tail)
        total = shares[0]
        for share in range(count - 1, 0, -1):
            mask = sum(1 << bit for k, bit in enumerate(group) if share >> (len(group) - 1 - k) & 1)
            total = total + swapped(shares[share].astype(jnp.bfloat16), mask, 1).astype(jnp.float32)
    return total


def solution(mesh):
    placed = (
        P(("groups", "trace", "space", "sub"), None, None),
        P("groups"),
        P("groups"),
        P(),
        P(),
        P(),
    )
    return jax.shard_map(
        per_device,
        mesh=mesh,
        in_specs=placed,
        out_specs=P(("groups", "trace", "space"), None, "sub", None),
        check_vma=False,
    )
```

```python
import functools
import math

import jax
import jax.numpy as jnp
import numpy as np
from jax import lax
from jax.experimental import pallas as pl
from jax.experimental.pallas import tpu as pltpu
from jax.sharding import PartitionSpec as P

SLAB = 32

def spectral_rows(freq_total, samples):
    quarter = freq_total // 4
    phase = (np.arange(quarter)[:, None] * np.arange(samples)[None, :]) % samples
    angle = phase.astype(np.float32) * np.float32(2.0 * math.pi / samples)
    factor = np.float32(1.0 / math.sqrt(samples))
    cosine, sine = np.cos(angle) * factor, -np.sin(angle) * factor
    step = np.arange(samples)
    size = np.where(step % 2 == 0, factor, np.cos(np.float32(math.pi / 4)) * factor)
    sine[0] = np.where(step // 4 % 2 == 0, size, -size)
    rows = np.concatenate([cosine, sine]).reshape(2 * quarter, samples // 4, 4)
    return rows.transpose(2, 0, 1).astype(jnp.bfloat16)


def halves(x):
    high = x.astype(jnp.bfloat16)
    return high, (x - high.astype(jnp.float32)).astype(jnp.bfloat16)


def exchange_groups(spaces, bands):
    space_bits, band_bits = spaces.bit_length() - 1, bands.bit_length() - 1
    bits = list(range(space_bits + band_bits))
    first = [bit for bit in (0, space_bits) if bit in bits and (bit == 0 or band_bits)]
    first = sorted(set(first))
    return [first] + [[bit] for bit in bits if bit not in first]


def place_of(delta, groups):
    order = [bit for group in groups for bit in group]
    place = 0
    for k, bit in enumerate(order):
        place = place | (((delta >> bit) & 1) << (len(order) - 1 - k))
    crossings = 0
    for group in groups:
        met = 0
        for bit in group:
            met = met | ((delta >> bit) & 1)
        crossings = crossings ^ met
    return place, crossings


def source_kernel(
    sizes,
    table_hbm,
    low_hbm,
    high_hbm,
    seismic_hbm,
    rows_hbm,
    leaf_hbm,
    moves_hbm,
    keep_ref,
    send_ref,
    table_ref,
    low_ref,
    high_ref,
    seismic_ref,
    wide_ref,
    rows_ref,
    leaf_ref,
    moves_ref,
    mask_ref,
    spectra_ref,
    first_high_ref,
    first_low_ref,
    second_high_ref,
    second_low_ref,
    sems,
):
    traces, samples, shots, freq_total, rank, bands, spaces, subs = sizes
    quarter = freq_total // 4
    freq_block = freq_total // bands
    boxes = bands * spaces
    box_bits = boxes.bit_length() - 1
    space_bits = spaces.bit_length() - 1
    part = rank // subs
    groups = exchange_groups(spaces, bands)
    own_space, own_sub = lax.axis_index("space"), lax.axis_index("sub")
    own_box = lax.axis_index("trace") * spaces + own_space

    copies = []
    for source, target in (
        [(low_hbm, low_ref), (high_hbm, high_ref)]
        + [(seismic_hbm.at[j], seismic_ref.at[j]) for j in range(2)]
        + [(rows_hbm, rows_ref)]
        + [(seismic_hbm.at[j], seismic_ref.at[j]) for j in range(2, traces)]
        + [(leaf_hbm, leaf_ref), (moves_hbm, moves_ref), (table_hbm, table_ref)]
    ):
        copy = pltpu.make_async_copy(source, target, sems.at[len(copies)])
        copy.start()
        copies.append(copy)
    low_copy, high_copy, rows_copy = copies[0], copies[1], copies[4]
    trace_copies, (leaf_copy, moves_copy, table_copy) = copies[2:4] + copies[5 : 3 + traces], copies[3 + traces :]

    low_copy.wait()
    high_copy.wait()
    row = lax.broadcasted_iota(jnp.int32, (quarter, shots), 0)
    mirrored = jnp.where(row == 0, 0, quarter - row)
    for q in range(4):
        freq = q * quarter + (mirrored if q % 2 else row)
        kept = (freq >= low_ref[...]) & (freq < high_ref[...])
        mask_ref[q] = jnp.where(kept, 1.0, 0.0).astype(jnp.bfloat16)
    top = lax.broadcasted_iota(jnp.int32, (SLAB, 2 * shots), 0) == 0

    arrivals = {0: traces // 4, traces // 4: traces // 2, traces // 2: traces}
    for j in range(0, traces, 2):
        if j in arrivals:
            for copy in trace_copies[j : arrivals[j]]:
                copy.wait()
        for k in range(2):
            wide_ref[j + k] = seismic_ref[j + k].astype(jnp.float32)
        if j == 0:
            rows_copy.wait()
        sums = []
        for r in range(4):
            pair = jnp.concatenate(
                [wide_ref[j + k, pl.ds(r, samples // 4, stride=4), :].astype(jnp.bfloat16) for k in range(2)], axis=1
            )
            sums.append(jnp.dot(rows_ref[r], pair, preferred_element_type=jnp.float32))
        for start in range(0, quarter, SLAB):
            cos = [x[start : start + SLAB] for x in sums]
            sin = [x[quarter + start : quarter + start + SLAB] for x in sums]
            extra = sin
            if start == 0:
                sin = [jnp.where(top, 0.0, x) for x in sin]
            even, odd, even_gap, odd_gap = cos[0] + cos[2], cos[1] + cos[3], cos[0] - cos[2], cos[3] - cos[1]
            s_even, s_odd, s_even_gap, s_odd_gap = sin[0] + sin[2], sin[1] + sin[3], sin[0] - sin[2], sin[1] - sin[3]
            real = [even + odd, even_gap - s_odd_gap, even_gap + s_odd_gap, even - odd]
            imag = [s_even + s_odd, odd_gap - s_even_gap, odd_gap + s_even_gap, s_odd - s_even]
            if start == 0:
                gap, both = extra[1] - extra[3], extra[1] + extra[3]
                real[1] = jnp.where(top, extra[0] + gap, real[1])
                imag[1] = jnp.where(top, -extra[2] - both, imag[1])
                real[3] = jnp.where(top, extra[0] - gap, real[3])
                imag[3] = jnp.where(top, extra[2] - both, imag[3])
            for q in range(4):
                for c, piece in enumerate((real[q], imag[q])):
                    piece = piece.astype(jnp.bfloat16)
                    for k in range(2):
                        spectra_ref[q, pl.ds((j + k) * quarter + start, SLAB), pl.ds(c * shots, shots)] = (
                            piece[:, k * shots : (k + 1) * shots]
                        )

    leaf_copy.wait()
    moves_copy.wait()
    table_copy.wait()
    lane = lax.broadcasted_iota(jnp.int32, (2 * rank, quarter), 1)
    flip = jnp.where(lane == 0, 0, quarter - lane)
    totals = [None] * bands
    for q in range(4):
        mask = jnp.concatenate([mask_ref[q]] * 2, axis=1)
        masked = jnp.concatenate([spectra_ref[q, pl.ds(j * quarter, quarter), :] * mask for j in range(traces)], axis=0)
        blocks = [leaf_ref[j, :, pl.ds(q * quarter, quarter)] for j in range(traces)]
        if q % 2:
            blocks = [jnp.take_along_axis(x.astype(jnp.float32), flip, axis=1).astype(jnp.bfloat16) for x in blocks]
        left = jnp.concatenate(blocks, axis=1)
        for g in range(q * quarter // freq_block, -(-(q + 1) * quarter // freq_block)):
            own = left
            if freq_block < quarter:
                lane = lax.broadcasted_iota(jnp.int32, left.shape, 1) % quarter
                freq = q * quarter + (jnp.where(lane == 0, 0, quarter - lane) if q % 2 else lane)
                own = jnp.where(freq // freq_block == g, left, jnp.zeros_like(left))
            total = jnp.dot(own, masked, preferred_element_type=jnp.float32)
            totals[g] = total if totals[g] is None else totals[g] + total

    def joined(product):
        real = product[:rank, :shots] - product[rank:, shots:]
        imag = product[rank:, :shots] + product[:rank, shots:]
        return jnp.concatenate([real, imag], axis=1)

    def store_in(refs):
        def store(box, value):
            refs[0][box], refs[1][box] = halves(value)

        return store

    def store_last(box, value):
        place, crossings = place_of(box ^ own_box, groups)
        first, second = (
            jnp.stack([value[half * part : (half + 1) * part, c * shots : (c + 1) * shots] for c in range(2)])
            for half in range(2)
        )
        keep_first = (own_sub ^ crossings) == 0
        keep_ref[place] = jnp.where(keep_first, first, second)
        send_ref[place] = jnp.where(keep_first, second, first).astype(jnp.bfloat16)

    held = [(first_high_ref, first_low_ref), (second_high_ref, second_low_ref)]
    for g in range(bands):
        store_in(held[0])(g, joined(totals[g]))

    def level(section_no, source, store):
        stride = 1 << section_no
        inside = section_no < space_bits
        count = bands * stride if inside else boxes // 2
        high_ref, low_ref = source

        def pair(i):
            if inside:
                done, band = i % stride, i // stride
                lower = band * spaces + ((own_space >> (section_no + 1)) << (section_no + 1)) + done
                own_bit = (own_space >> section_no) & 1
                children, held_at = [own_bit, own_bit], [i]
                places = [band * (2 * stride) + upper * stride + done for upper in range(2)]
            else:
                lower = (i // stride) * (2 * stride) + i % stride
                children, held_at = [0, 1], [lower, lower + stride]
                places = [lower, lower + stride]
            entries = [[table_ref[section_no, child, lower + upper * stride] for child in children] for upper in range(2)]
            left = jnp.concatenate(
                [
                    jnp.concatenate([moves_ref[entry, c] for entry in entries[upper]], axis=1)
                    for upper in range(2)
                    for c in range(2)
                ],
                axis=0,
            )
            high = left.astype(jnp.bfloat16)
            rest = left - high.astype(jnp.float32)
            right_high = [high_ref[k] for k in held_at]
            right_low = [low_ref[k] for k in held_at]
            if inside:
                lane = lax.broadcasted_iota(jnp.int32, left.shape, 1)
                left = [jnp.where(lane < rank, high.astype(jnp.float32), rest).astype(jnp.bfloat16), high]
                right = right_high * 2 + right_low + [jnp.zeros_like(right_low[0])]
            else:
                left = [high, rest.astype(jnp.bfloat16), high]
                right = right_high * 2 + right_low
            product = jnp.dot(
                jnp.concatenate(left, axis=1), jnp.concatenate(right, axis=0), preferred_element_type=jnp.float32
            )
            for upper in range(2):
                store(places[upper], joined(product[upper * 2 * rank : (upper + 1) * 2 * rank]))

        if count <= 4:
            for i in range(count):
                pair(i)
        else:
            lax.fori_loop(0, count, lambda i, carry: (pair(i), carry)[1], 0)

    for section_no in range(box_bits):
        last = section_no == box_bits - 1
        level(section_no, held[section_no % 2], store_last if last else store_in(held[(section_no + 1) % 2]))


def per_device(seismic, band_low, band_high, leaf_weights, translations, level_table):
    bands, spaces, subs = (lax.axis_size(name) for name in ("trace", "space", "sub"))
    traces, samples, shots = seismic.shape
    freq_total, rank = leaf_weights.shape[1], leaf_weights.shape[3]
    boxes = bands * spaces
    rows = jnp.asarray(spectral_rows(freq_total, samples))
    leaf = leaf_weights.transpose(0, 2, 3, 1).reshape(traces, 2 * rank, freq_total)
    tail = (2, rank // subs, shots)
    kind = pltpu.VMEM if boxes * 2 * rank * shots <= 1 << 18 else jax.ShapeDtypeStruct
    vmem = pl.BlockSpec(memory_space=pltpu.VMEM)
    anywhere = pl.BlockSpec(memory_space=pl.ANY)
    keep, send = pl.pallas_call(
        functools.partial(source_kernel, (traces, samples, shots, freq_total, rank, bands, spaces, subs)),
        out_shape=(
            kind((boxes,) + tail, jnp.float32),
            kind((boxes,) + tail, jnp.bfloat16),
        ),
        in_specs=[anywhere] * 7,
        out_specs=(vmem, vmem),
        scratch_shapes=[
            pltpu.SMEM((level_table.shape[0], 2, boxes), jnp.int32),
            pltpu.VMEM((1, shots), jnp.int32),
            pltpu.VMEM((1, shots), jnp.int32),
            pltpu.VMEM(seismic.shape, jnp.bfloat16),
            pltpu.VMEM(seismic.shape, jnp.float32),
            pltpu.VMEM(rows.shape, jnp.bfloat16),
            pltpu.VMEM(leaf.shape, jnp.bfloat16),
            pltpu.VMEM(translations.shape, jnp.float32),
            pltpu.VMEM((4, freq_total // 4, shots), jnp.bfloat16),
            pltpu.VMEM((4, traces * freq_total // 4, 2 * shots), jnp.bfloat16),
        ]
        + [pltpu.VMEM((boxes, rank, 2 * shots), jnp.bfloat16)] * 4
        + [pltpu.SemaphoreType.DMA((traces + 6,))],
        name="source",
    )(
        level_table.transpose(0, 2, 1),
        band_low[None, :],
        band_high[None, :],
        seismic,
        rows,
        leaf,
        translations,
    )

    axes = ("trace", "space", "sub")

    def swapped(x, mask, flip):
        return lax.ppermute(x, axes, [(i, ((i >> 1 ^ mask) << 1) | (i & 1 ^ flip)) for i in range(2 * boxes)])

    total = keep + swapped(send, 0, 1).astype(jnp.float32)
    for group in exchange_groups(spaces, bands):
        count = 1 << len(group)
        shares = total.reshape((count, -1) + tail)
        total = shares[0]
        for share in range(count - 1, 0, -1):
            mask = sum(1 << bit for k, bit in enumerate(group) if share >> (len(group) - 1 - k) & 1)
            total = total + swapped(shares[share].astype(jnp.bfloat16), mask, 1).astype(jnp.float32)
    return total


def solution(mesh):
    placed = (
        P(("groups", "trace", "space", "sub"), None, None),
        P("groups"),
        P("groups"),
        P(),
        P(),
        P(),
    )
    return jax.shard_map(
        per_device,
        mesh=mesh,
        in_specs=placed,
        out_specs=P(("groups", "trace", "space"), None, "sub", None),
        check_vma=False,
    )
```

```python
import functools
import math

import jax
import jax.numpy as jnp
import numpy as np
from jax import lax
from jax.experimental import pallas as pl
from jax.experimental.pallas import tpu as pltpu
from jax.sharding import PartitionSpec as P

SLAB = 32

def spectral_rows(freq_total, samples):
    quarter = freq_total // 4
    phase = (np.arange(quarter)[:, None] * np.arange(samples)[None, :]) % samples
    angle = phase.astype(np.float32) * np.float32(2.0 * math.pi / samples)
    factor = np.float32(1.0 / math.sqrt(samples))
    cosine, sine = np.cos(angle) * factor, -np.sin(angle) * factor
    step = np.arange(samples)
    size = np.where(step % 2 == 0, factor, np.cos(np.float32(math.pi / 4)) * factor)
    sine[0] = np.where(step // 4 % 2 == 0, size, -size)
    rows = np.concatenate([cosine, sine]).reshape(2 * quarter, samples // 4, 4)
    return rows.transpose(2, 0, 1).astype(jnp.bfloat16)


def halves(x):
    high = x.astype(jnp.bfloat16)
    return high, (x - high.astype(jnp.float32)).astype(jnp.bfloat16)


def exchange_groups(spaces, bands):
    space_bits, band_bits = spaces.bit_length() - 1, bands.bit_length() - 1
    bits = list(range(space_bits + band_bits))
    first = [bit for bit in (0, space_bits) if bit in bits and (bit == 0 or band_bits)]
    first = sorted(set(first))
    return [first] + [[bit] for bit in bits if bit not in first]


def place_of(delta, groups):
    order = [bit for group in groups for bit in group]
    place = 0
    for k, bit in enumerate(order):
        place = place | (((delta >> bit) & 1) << (len(order) - 1 - k))
    crossings = 0
    for group in groups:
        met = 0
        for bit in group:
            met = met | ((delta >> bit) & 1)
        crossings = crossings ^ met
    return place, crossings


def source_kernel(
    sizes,
    table_hbm,
    low_hbm,
    high_hbm,
    seismic_hbm,
    rows_hbm,
    leaf_hbm,
    moves_hbm,
    keep_ref,
    send_ref,
    table_ref,
    low_ref,
    high_ref,
    seismic_ref,
    wide_ref,
    rows_ref,
    leaf_ref,
    moves_ref,
    mask_ref,
    spectra_ref,
    first_high_ref,
    first_low_ref,
    second_high_ref,
    second_low_ref,
    sems,
):
    traces, samples, shots, freq_total, rank, bands, spaces, subs = sizes
    quarter = freq_total // 4
    freq_block = freq_total // bands
    boxes = bands * spaces
    box_bits = boxes.bit_length() - 1
    space_bits = spaces.bit_length() - 1
    part = rank // subs
    groups = exchange_groups(spaces, bands)
    own_space, own_sub = lax.axis_index("space"), lax.axis_index("sub")
    own_box = lax.axis_index("trace") * spaces + own_space

    copies = []
    for source, target in (
        [(low_hbm, low_ref), (high_hbm, high_ref)]
        + [(seismic_hbm.at[j], seismic_ref.at[j]) for j in range(2)]
        + [(rows_hbm, rows_ref)]
        + [(seismic_hbm.at[j], seismic_ref.at[j]) for j in range(2, traces)]
        + [(moves_hbm, moves_ref), (table_hbm, table_ref), (leaf_hbm, leaf_ref)]
    ):
        copy = pltpu.make_async_copy(source, target, sems.at[len(copies)])
        copy.start()
        copies.append(copy)
    low_copy, high_copy, rows_copy = copies[0], copies[1], copies[4]
    trace_copies, (moves_copy, table_copy, leaf_copy) = copies[2:4] + copies[5 : 3 + traces], copies[3 + traces :]

    low_copy.wait()
    high_copy.wait()
    row = lax.broadcasted_iota(jnp.int32, (quarter, shots), 0)
    mirrored = jnp.where(row == 0, 0, quarter - row)
    for q in range(4):
        freq = q * quarter + (mirrored if q % 2 else row)
        kept = (freq >= low_ref[...]) & (freq < high_ref[...])
        mask_ref[q] = jnp.where(kept, 1.0, 0.0).astype(jnp.bfloat16)
    top = lax.broadcasted_iota(jnp.int32, (SLAB, 2 * shots), 0) == 0

    arrivals = {0: traces // 4, traces // 4: traces // 2, traces // 2: traces}
    for j in range(0, traces, 2):
        if j in arrivals:
            for copy in trace_copies[j : arrivals[j]]:
                copy.wait()
        for k in range(2):
            wide_ref[j + k] = seismic_ref[j + k].astype(jnp.float32)
        if j == 0:
            rows_copy.wait()
        sums = []
        for r in range(4):
            pair = jnp.concatenate(
                [wide_ref[j + k, pl.ds(r, samples // 4, stride=4), :].astype(jnp.bfloat16) for k in range(2)], axis=1
            )
            sums.append(jnp.dot(rows_ref[r], pair, preferred_element_type=jnp.float32))
        for start in range(0, quarter, SLAB):
            cos = [x[start : start + SLAB] for x in sums]
            sin = [x[quarter + start : quarter + start + SLAB] for x in sums]
            extra = sin
            if start == 0:
                sin = [jnp.where(top, 0.0, x) for x in sin]
            even, odd, even_gap, odd_gap = cos[0] + cos[2], cos[1] + cos[3], cos[0] - cos[2], cos[3] - cos[1]
            s_even, s_odd, s_even_gap, s_odd_gap = sin[0] + sin[2], sin[1] + sin[3], sin[0] - sin[2], sin[1] - sin[3]
            real = [even + odd, even_gap - s_odd_gap, even_gap + s_odd_gap, even - odd]
            imag = [s_even + s_odd, odd_gap - s_even_gap, odd_gap + s_even_gap, s_odd - s_even]
            if start == 0:
                gap, both = extra[1] - extra[3], extra[1] + extra[3]
                real[1] = jnp.where(top, extra[0] + gap, real[1])
                imag[1] = jnp.where(top, -extra[2] - both, imag[1])
                real[3] = jnp.where(top, extra[0] - gap, real[3])
                imag[3] = jnp.where(top, extra[2] - both, imag[3])
            for q in range(4):
                for c, piece in enumerate((real[q], imag[q])):
                    piece = piece.astype(jnp.bfloat16)
                    for k in range(2):
                        spectra_ref[q, pl.ds((j + k) * quarter + start, SLAB), pl.ds(c * shots, shots)] = (
                            piece[:, k * shots : (k + 1) * shots]
                        )

    leaf_copy.wait()
    moves_copy.wait()
    table_copy.wait()
    lane = lax.broadcasted_iota(jnp.int32, (2 * rank, quarter), 1)
    flip = jnp.where(lane == 0, 0, quarter - lane)
    totals = [None] * bands
    for q in range(4):
        mask = jnp.concatenate([mask_ref[q]] * 2, axis=1)
        masked = jnp.concatenate([spectra_ref[q, pl.ds(j * quarter, quarter), :] * mask for j in range(traces)], axis=0)
        blocks = [leaf_ref[j, :, pl.ds(q * quarter, quarter)] for j in range(traces)]
        if q % 2:
            blocks = [jnp.take_along_axis(x.astype(jnp.float32), flip, axis=1).astype(jnp.bfloat16) for x in blocks]
        left = jnp.concatenate(blocks, axis=1)
        for g in range(q * quarter // freq_block, -(-(q + 1) * quarter // freq_block)):
            own = left
            if freq_block < quarter:
                lane = lax.broadcasted_iota(jnp.int32, left.shape, 1) % quarter
                freq = q * quarter + (jnp.where(lane == 0, 0, quarter - lane) if q % 2 else lane)
                own = jnp.where(freq // freq_block == g, left, jnp.zeros_like(left))
            total = jnp.dot(own, masked, preferred_element_type=jnp.float32)
            totals[g] = total if totals[g] is None else totals[g] + total

    def joined(product):
        real = product[:rank, :shots] - product[rank:, shots:]
        imag = product[rank:, :shots] + product[:rank, shots:]
        return jnp.concatenate([real, imag], axis=1)

    def store_in(refs):
        def store(box, value):
            refs[0][box], refs[1][box] = halves(value)

        return store

    def store_last(box, value):
        place, crossings = place_of(box ^ own_box, groups)
        first, second = (
            jnp.stack([value[half * part : (half + 1) * part, c * shots : (c + 1) * shots] for c in range(2)])
            for half in range(2)
        )
        keep_first = (own_sub ^ crossings) == 0
        keep_ref[place] = jnp.where(keep_first, first, second)
        send_ref[place] = jnp.where(keep_first, second, first).astype(jnp.bfloat16)

    held = [(first_high_ref, first_low_ref), (second_high_ref, second_low_ref)]
    for g in range(bands):
        store_in(held[0])(g, joined(totals[g]))

    def level(section_no, source, store):
        stride = 1 << section_no
        inside = section_no < space_bits
        count = bands * stride if inside else boxes // 2
        high_ref, low_ref = source

        def pair(i):
            if inside:
                done, band = i % stride, i // stride
                lower = band * spaces + ((own_space >> (section_no + 1)) << (section_no + 1)) + done
                own_bit = (own_space >> section_no) & 1
                children, held_at = [own_bit, own_bit], [i]
                places = [band * (2 * stride) + upper * stride + done for upper in range(2)]
            else:
                lower = (i // stride) * (2 * stride) + i % stride
                children, held_at = [0, 1], [lower, lower + stride]
                places = [lower, lower + stride]
            entries = [[table_ref[section_no, child, lower + upper * stride] for child in children] for upper in range(2)]
            left = jnp.concatenate(
                [
                    jnp.concatenate([moves_ref[entry, c] for entry in entries[upper]], axis=1)
                    for upper in range(2)
                    for c in range(2)
                ],
                axis=0,
            )
            high = left.astype(jnp.bfloat16)
            rest = left - high.astype(jnp.float32)
            right_high = [high_ref[k] for k in held_at]
            right_low = [low_ref[k] for k in held_at]
            if inside:
                lane = lax.broadcasted_iota(jnp.int32, left.shape, 1)
                left = [jnp.where(lane < rank, high.astype(jnp.float32), rest).astype(jnp.bfloat16), high]
                right = right_high * 2 + right_low + [jnp.zeros_like(right_low[0])]
            else:
                left = [high, rest.astype(jnp.bfloat16), high]
                right = right_high * 2 + right_low
            product = jnp.dot(
                jnp.concatenate(left, axis=1), jnp.concatenate(right, axis=0), preferred_element_type=jnp.float32
            )
            for upper in range(2):
                store(places[upper], joined(product[upper * 2 * rank : (upper + 1) * 2 * rank]))

        if count <= 4:
            for i in range(count):
                pair(i)
        else:
            lax.fori_loop(0, count, lambda i, carry: (pair(i), carry)[1], 0)

    for section_no in range(box_bits):
        last = section_no == box_bits - 1
        level(section_no, held[section_no % 2], store_last if last else store_in(held[(section_no + 1) % 2]))


def per_device(seismic, band_low, band_high, leaf_weights, translations, level_table):
    bands, spaces, subs = (lax.axis_size(name) for name in ("trace", "space", "sub"))
    traces, samples, shots = seismic.shape
    freq_total, rank = leaf_weights.shape[1], leaf_weights.shape[3]
    boxes = bands * spaces
    rows = jnp.asarray(spectral_rows(freq_total, samples))
    leaf = leaf_weights.transpose(0, 2, 3, 1).reshape(traces, 2 * rank, freq_total)
    tail = (2, rank // subs, shots)
    kind = pltpu.VMEM if boxes * 2 * rank * shots <= 1 << 18 else jax.ShapeDtypeStruct
    vmem = pl.BlockSpec(memory_space=pltpu.VMEM)
    anywhere = pl.BlockSpec(memory_space=pl.ANY)
    keep, send = pl.pallas_call(
        functools.partial(source_kernel, (traces, samples, shots, freq_total, rank, bands, spaces, subs)),
        out_shape=(
            kind((boxes,) + tail, jnp.float32),
            kind((boxes,) + tail, jnp.bfloat16),
        ),
        in_specs=[anywhere] * 7,
        out_specs=(vmem, vmem),
        scratch_shapes=[
            pltpu.SMEM((level_table.shape[0], 2, boxes), jnp.int32),
            pltpu.VMEM((1, shots), jnp.int32),
            pltpu.VMEM((1, shots), jnp.int32),
            pltpu.VMEM(seismic.shape, jnp.bfloat16),
            pltpu.VMEM(seismic.shape, jnp.float32),
            pltpu.VMEM(rows.shape, jnp.bfloat16),
            pltpu.VMEM(leaf.shape, jnp.bfloat16),
            pltpu.VMEM(translations.shape, jnp.float32),
            pltpu.VMEM((4, freq_total // 4, shots), jnp.bfloat16),
            pltpu.VMEM((4, traces * freq_total // 4, 2 * shots), jnp.bfloat16),
        ]
        + [pltpu.VMEM((boxes, rank, 2 * shots), jnp.bfloat16)] * 4
        + [pltpu.SemaphoreType.DMA((traces + 6,))],
        name="source",
    )(
        level_table.transpose(0, 2, 1),
        band_low[None, :],
        band_high[None, :],
        seismic,
        rows,
        leaf,
        translations,
    )

    axes = ("trace", "space", "sub")

    def swapped(x, mask, flip):
        return lax.ppermute(x, axes, [(i, ((i >> 1 ^ mask) << 1) | (i & 1 ^ flip)) for i in range(2 * boxes)])

    total = keep + swapped(send, 0, 1).astype(jnp.float32)
    for group in exchange_groups(spaces, bands):
        count = 1 << len(group)
        shares = total.reshape((count, -1) + tail)
        total = shares[0]
        for share in range(count - 1, 0, -1):
            mask = sum(1 << bit for k, bit in enumerate(group) if share >> (len(group) - 1 - k) & 1)
            total = total + swapped(shares[share].astype(jnp.bfloat16), mask, 1).astype(jnp.float32)
    return total


def solution(mesh):
    placed = (
        P(("groups", "trace", "space", "sub"), None, None),
        P("groups"),
        P("groups"),
        P(),
        P(),
        P(),
    )
    return jax.shard_map(
        per_device,
        mesh=mesh,
        in_specs=placed,
        out_specs=P(("groups", "trace", "space"), None, "sub", None),
        check_vma=False,
    )
```

```python
import functools
import math

import jax
import jax.numpy as jnp
import numpy as np
from jax import lax
from jax.experimental import pallas as pl
from jax.experimental.pallas import tpu as pltpu
from jax.sharding import PartitionSpec as P

SLAB = 64

def spectral_rows(freq_total, samples):
    quarter = freq_total // 4
    phase = (np.arange(quarter)[:, None] * np.arange(samples)[None, :]) % samples
    angle = phase.astype(np.float32) * np.float32(2.0 * math.pi / samples)
    factor = np.float32(1.0 / math.sqrt(samples))
    cosine, sine = np.cos(angle) * factor, -np.sin(angle) * factor
    step = np.arange(samples)
    size = np.where(step % 2 == 0, factor, np.cos(np.float32(math.pi / 4)) * factor)
    sine[0] = np.where(step // 4 % 2 == 0, size, -size)
    rows = np.concatenate([cosine, sine]).reshape(2 * quarter, samples // 4, 4)
    return rows.transpose(2, 0, 1).astype(jnp.bfloat16)


def halves(x):
    high = x.astype(jnp.bfloat16)
    return high, (x - high.astype(jnp.float32)).astype(jnp.bfloat16)


def exchange_groups(spaces, bands):
    space_bits, band_bits = spaces.bit_length() - 1, bands.bit_length() - 1
    bits = list(range(space_bits + band_bits))
    first = [bit for bit in (0, space_bits) if bit in bits and (bit == 0 or band_bits)]
    first = sorted(set(first))
    return [first] + [[bit] for bit in bits if bit not in first]


def place_of(delta, groups):
    order = [bit for group in groups for bit in group]
    place = 0
    for k, bit in enumerate(order):
        place = place | (((delta >> bit) & 1) << (len(order) - 1 - k))
    crossings = 0
    for group in groups:
        met = 0
        for bit in group:
            met = met | ((delta >> bit) & 1)
        crossings = crossings ^ met
    return place, crossings


def source_kernel(
    sizes,
    table_hbm,
    low_hbm,
    high_hbm,
    seismic_hbm,
    rows_hbm,
    leaf_hbm,
    moves_hbm,
    keep_ref,
    send_ref,
    table_ref,
    low_ref,
    high_ref,
    seismic_ref,
    wide_ref,
    rows_ref,
    leaf_ref,
    moves_ref,
    mask_ref,
    spectra_ref,
    first_high_ref,
    first_low_ref,
    second_high_ref,
    second_low_ref,
    sems,
):
    traces, samples, shots, freq_total, rank, bands, spaces, subs = sizes
    quarter = freq_total // 4
    freq_block = freq_total // bands
    boxes = bands * spaces
    box_bits = boxes.bit_length() - 1
    space_bits = spaces.bit_length() - 1
    part = rank // subs
    groups = exchange_groups(spaces, bands)
    own_space, own_sub = lax.axis_index("space"), lax.axis_index("sub")
    own_box = lax.axis_index("trace") * spaces + own_space

    copies = []
    for source, target in (
        [(low_hbm, low_ref), (high_hbm, high_ref)]
        + [(seismic_hbm.at[j], seismic_ref.at[j]) for j in range(2)]
        + [(rows_hbm, rows_ref)]
        + [(seismic_hbm.at[j], seismic_ref.at[j]) for j in range(2, traces)]
        + [(moves_hbm, moves_ref), (table_hbm, table_ref), (leaf_hbm, leaf_ref)]
    ):
        copy = pltpu.make_async_copy(source, target, sems.at[len(copies)])
        copy.start()
        copies.append(copy)
    low_copy, high_copy, rows_copy = copies[0], copies[1], copies[4]
    trace_copies, (moves_copy, table_copy, leaf_copy) = copies[2:4] + copies[5 : 3 + traces], copies[3 + traces :]

    low_copy.wait()
    high_copy.wait()
    row = lax.broadcasted_iota(jnp.int32, (quarter, shots), 0)
    mirrored = jnp.where(row == 0, 0, quarter - row)
    for q in range(4):
        freq = q * quarter + (mirrored if q % 2 else row)
        kept = (freq >= low_ref[...]) & (freq < high_ref[...])
        mask_ref[q] = jnp.where(kept, 1.0, 0.0).astype(jnp.bfloat16)
    top = lax.broadcasted_iota(jnp.int32, (SLAB, 2 * shots), 0) == 0

    arrivals = {0: traces // 4, traces // 4: traces // 2, traces // 2: traces}
    for j in range(0, traces, 2):
        if j in arrivals:
            for copy in trace_copies[j : arrivals[j]]:
                copy.wait()
        for k in range(2):
            wide_ref[j + k] = seismic_ref[j + k].astype(jnp.float32)
        if j == 0:
            rows_copy.wait()
        sums = []
        for r in range(4):
            pair = jnp.concatenate(
                [wide_ref[j + k, pl.ds(r, samples // 4, stride=4), :].astype(jnp.bfloat16) for k in range(2)], axis=1
            )
            sums.append(jnp.dot(rows_ref[r], pair, preferred_element_type=jnp.float32))
        for start in range(0, quarter, SLAB):
            cos = [x[start : start + SLAB] for x in sums]
            sin = [x[quarter + start : quarter + start + SLAB] for x in sums]
            extra = sin
            if start == 0:
                sin = [jnp.where(top, 0.0, x) for x in sin]
            even, odd, even_gap, odd_gap = cos[0] + cos[2], cos[1] + cos[3], cos[0] - cos[2], cos[3] - cos[1]
            s_even, s_odd, s_even_gap, s_odd_gap = sin[0] + sin[2], sin[1] + sin[3], sin[0] - sin[2], sin[1] - sin[3]
            real = [even + odd, even_gap - s_odd_gap, even_gap + s_odd_gap, even - odd]
            imag = [s_even + s_odd, odd_gap - s_even_gap, odd_gap + s_even_gap, s_odd - s_even]
            if start == 0:
                gap, both = extra[1] - extra[3], extra[1] + extra[3]
                real[1] = jnp.where(top, extra[0] + gap, real[1])
                imag[1] = jnp.where(top, -extra[2] - both, imag[1])
                real[3] = jnp.where(top, extra[0] - gap, real[3])
                imag[3] = jnp.where(top, extra[2] - both, imag[3])
            for q in range(4):
                for c, piece in enumerate((real[q], imag[q])):
                    piece = piece.astype(jnp.bfloat16)
                    for k in range(2):
                        spectra_ref[q, pl.ds((j + k) * quarter + start, SLAB), pl.ds(c * shots, shots)] = (
                            piece[:, k * shots : (k + 1) * shots]
                        )

    leaf_copy.wait()
    moves_copy.wait()
    table_copy.wait()
    lane = lax.broadcasted_iota(jnp.int32, (2 * rank, quarter), 1)
    flip = jnp.where(lane == 0, 0, quarter - lane)
    totals = [None] * bands
    for q in range(4):
        mask = jnp.concatenate([mask_ref[q]] * 2, axis=1)
        masked = jnp.concatenate([spectra_ref[q, pl.ds(j * quarter, quarter), :] * mask for j in range(traces)], axis=0)
        blocks = [leaf_ref[j, :, pl.ds(q * quarter, quarter)] for j in range(traces)]
        if q % 2:
            blocks = [jnp.take_along_axis(x.astype(jnp.float32), flip, axis=1).astype(jnp.bfloat16) for x in blocks]
        left = jnp.concatenate(blocks, axis=1)
        for g in range(q * quarter // freq_block, -(-(q + 1) * quarter // freq_block)):
            own = left
            if freq_block < quarter:
                lane = lax.broadcasted_iota(jnp.int32, left.shape, 1) % quarter
                freq = q * quarter + (jnp.where(lane == 0, 0, quarter - lane) if q % 2 else lane)
                own = jnp.where(freq // freq_block == g, left, jnp.zeros_like(left))
            total = jnp.dot(own, masked, preferred_element_type=jnp.float32)
            totals[g] = total if totals[g] is None else totals[g] + total

    def joined(product):
        real = product[:rank, :shots] - product[rank:, shots:]
        imag = product[rank:, :shots] + product[:rank, shots:]
        return jnp.concatenate([real, imag], axis=1)

    def store_in(refs):
        def store(box, value):
            refs[0][box], refs[1][box] = halves(value)

        return store

    def store_last(box, value):
        place, crossings = place_of(box ^ own_box, groups)
        first, second = (
            jnp.stack([value[half * part : (half + 1) * part, c * shots : (c + 1) * shots] for c in range(2)])
            for half in range(2)
        )
        keep_first = (own_sub ^ crossings) == 0
        keep_ref[place] = jnp.where(keep_first, first, second)
        send_ref[place] = jnp.where(keep_first, second, first).astype(jnp.bfloat16)

    held = [(first_high_ref, first_low_ref), (second_high_ref, second_low_ref)]
    for g in range(bands):
        store_in(held[0])(g, joined(totals[g]))

    def level(section_no, source, store):
        stride = 1 << section_no
        inside = section_no < space_bits
        count = bands * stride if inside else boxes // 2
        high_ref, low_ref = source

        def pair(i):
            if inside:
                done, band = i % stride, i // stride
                lower = band * spaces + ((own_space >> (section_no + 1)) << (section_no + 1)) + done
                own_bit = (own_space >> section_no) & 1
                children, held_at = [own_bit, own_bit], [i]
                places = [band * (2 * stride) + upper * stride + done for upper in range(2)]
            else:
                lower = (i // stride) * (2 * stride) + i % stride
                children, held_at = [0, 1], [lower, lower + stride]
                places = [lower, lower + stride]
            entries = [[table_ref[section_no, child, lower + upper * stride] for child in children] for upper in range(2)]
            left = jnp.concatenate(
                [
                    jnp.concatenate([moves_ref[entry, c] for entry in entries[upper]], axis=1)
                    for upper in range(2)
                    for c in range(2)
                ],
                axis=0,
            )
            high = left.astype(jnp.bfloat16)
            rest = left - high.astype(jnp.float32)
            right_high = [high_ref[k] for k in held_at]
            right_low = [low_ref[k] for k in held_at]
            if inside:
                lane = lax.broadcasted_iota(jnp.int32, left.shape, 1)
                left = [jnp.where(lane < rank, high.astype(jnp.float32), rest).astype(jnp.bfloat16), high]
                right = right_high * 2 + right_low + [jnp.zeros_like(right_low[0])]
            else:
                left = [high, rest.astype(jnp.bfloat16), high]
                right = right_high * 2 + right_low
            product = jnp.dot(
                jnp.concatenate(left, axis=1), jnp.concatenate(right, axis=0), preferred_element_type=jnp.float32
            )
            for upper in range(2):
                store(places[upper], joined(product[upper * 2 * rank : (upper + 1) * 2 * rank]))

        if count <= 4:
            for i in range(count):
                pair(i)
        else:
            lax.fori_loop(0, count, lambda i, carry: (pair(i), carry)[1], 0)

    for section_no in range(box_bits):
        last = section_no == box_bits - 1
        level(section_no, held[section_no % 2], store_last if last else store_in(held[(section_no + 1) % 2]))


def per_device(seismic, band_low, band_high, leaf_weights, translations, level_table):
    bands, spaces, subs = (lax.axis_size(name) for name in ("trace", "space", "sub"))
    traces, samples, shots = seismic.shape
    freq_total, rank = leaf_weights.shape[1], leaf_weights.shape[3]
    boxes = bands * spaces
    rows = jnp.asarray(spectral_rows(freq_total, samples))
    leaf = leaf_weights.transpose(0, 2, 3, 1).reshape(traces, 2 * rank, freq_total)
    tail = (2, rank // subs, shots)
    kind = pltpu.VMEM if boxes * 2 * rank * shots <= 1 << 18 else jax.ShapeDtypeStruct
    vmem = pl.BlockSpec(memory_space=pltpu.VMEM)
    anywhere = pl.BlockSpec(memory_space=pl.ANY)
    keep, send = pl.pallas_call(
        functools.partial(source_kernel, (traces, samples, shots, freq_total, rank, bands, spaces, subs)),
        out_shape=(
            kind((boxes,) + tail, jnp.float32),
            kind((boxes,) + tail, jnp.bfloat16),
        ),
        in_specs=[anywhere] * 7,
        out_specs=(vmem, vmem),
        scratch_shapes=[
            pltpu.SMEM((level_table.shape[0], 2, boxes), jnp.int32),
            pltpu.VMEM((1, shots), jnp.int32),
            pltpu.VMEM((1, shots), jnp.int32),
            pltpu.VMEM(seismic.shape, jnp.bfloat16),
            pltpu.VMEM(seismic.shape, jnp.float32),
            pltpu.VMEM(rows.shape, jnp.bfloat16),
            pltpu.VMEM(leaf.shape, jnp.bfloat16),
            pltpu.VMEM(translations.shape, jnp.float32),
            pltpu.VMEM((4, freq_total // 4, shots), jnp.bfloat16),
            pltpu.VMEM((4, traces * freq_total // 4, 2 * shots), jnp.bfloat16),
        ]
        + [pltpu.VMEM((boxes, rank, 2 * shots), jnp.bfloat16)] * 4
        + [pltpu.SemaphoreType.DMA((traces + 6,))],
        name="source",
    )(
        level_table.transpose(0, 2, 1),
        band_low[None, :],
        band_high[None, :],
        seismic,
        rows,
        leaf,
        translations,
    )

    axes = ("trace", "space", "sub")

    def swapped(x, mask, flip):
        return lax.ppermute(x, axes, [(i, ((i >> 1 ^ mask) << 1) | (i & 1 ^ flip)) for i in range(2 * boxes)])

    total = keep + swapped(send, 0, 1).astype(jnp.float32)
    for group in exchange_groups(spaces, bands):
        count = 1 << len(group)
        shares = total.reshape((count, -1) + tail)
        total = shares[0]
        for share in range(count - 1, 0, -1):
            mask = sum(1 << bit for k, bit in enumerate(group) if share >> (len(group) - 1 - k) & 1)
            total = total + swapped(shares[share].astype(jnp.bfloat16), mask, 1).astype(jnp.float32)
    return total


def solution(mesh):
    placed = (
        P(("groups", "trace", "space", "sub"), None, None),
        P("groups"),
        P("groups"),
        P(),
        P(),
        P(),
    )
    return jax.shard_map(
        per_device,
        mesh=mesh,
        in_specs=placed,
        out_specs=P(("groups", "trace", "space"), None, "sub", None),
        check_vma=False,
    )
```
